32 devices in a mesh: freq: 16 (over z, y, x), seg: 2 (over core).
Axes of the slice: x: 2, y: 2, z: 4, core: 2. Of those that a mesh axis runs over, the one named last changes fastest.
Arguments:
- activity: float32 [64, 8, 64, 512], P('freq'), may hold values from 0.2 to 5
- system: float32 [2, 64, 2, 512, 512], P('seg', 'freq'), may hold values from -0.25 to 0.25
- pattern: int32 [2, 64, 4, 4], P('seg', 'freq'), may hold values 0 or 1
- counts: int32 [2, 64, 8, 64, 512], P('seg', 'freq'), may hold values from 0 to 15
- background: float32 [2, 64, 8, 64, 512], P('seg', 'freq'), may hold values from 1 to 4
- sensitivity: float32 [64, 64, 512], P('freq', 'seg'), may hold values from 0.5 to 4
Outputs:
- updated: float32 [64, 8, 64, 512], P('freq', None, 'seg')
The draws below stay inside these ranges and needn't reach their ends.
Inputs may be any that keep to these rules, and one draw needn't show every extreme that they name: `pattern`: 1 where a tile of a Fourier block is stored, 0 where the tile is zero.
All inputs are finite; a program needn't handle non-finite values.
Results may differ from the reference program's by a relative error of at most 0.0001.
Values sent between devices are 32-bit elements; how exact they have to be, the bound alone decides.
No kernel may reach another device: no remote copies, remote signals or barrier semaphores. Data moves between devices by JAX's collectives and lax.ppermute only.
A program may use at most 128 MiB of HBM per device.

```python
import math
import jax
import jax.numpy as jnp
from jax import lax

SECTORS = 64
TILE = 128
FRAMES = 8
PLANES = 64
IMG = 512
SINO = 512
SUBSETS = 2
N_SEG = 2


def set_ends(values, key, low, largest):
    longest = values.shape.index(max(values.shape))
    spots = []
    for shift in (0, 1):
        where = [jax.random.randint(jax.random.fold_in(key, axis), (), 0, length) for axis, length in enumerate(values.shape)]
        where[longest] = (where[longest] + shift) % values.shape[longest]
        spots.append(tuple(where))
    return values.at[spots[0]].set(low).at[spots[1]].set(largest)


def level_of(rng, dims, shards, low, largest):
    factor_of = 1.0
    for axis_at, parts in shards:
        heights = jax.random.uniform(jax.random.fold_in(jax.random.fold_in(rng, 6), axis_at), (parts,), jnp.float32, low / len(shards), largest / len(shards))
        factor_of = factor_of * jnp.repeat(jnp.exp(heights), dims[axis_at] // parts).reshape((-1,) + (1,) * (len(dims) - 1 - axis_at))
    return factor_of


def gaussian(stream_key, dims, deviation, bound, split=(), dtype=jnp.bfloat16):
    level = level_of(stream_key, dims, split, -0.22, 0.18) if split else 1.0
    array = jax.random.normal(stream_key, dims, jnp.float32) * deviation * level
    return jnp.minimum(jnp.maximum(array, -bound), bound).astype(dtype)


def setup_inputs(seed: int = 0) -> dict:
    seeds = jax.random.split(jax.random.key(seed), 7)
    return {
        "activity": jnp.clip(jnp.exp(math.log(5.0) - 3.218876 * jax.random.uniform(seeds[0], (SECTORS, FRAMES, PLANES, IMG), jnp.float32) ** level_of(seeds[0], (SECTORS, FRAMES, PLANES, IMG), ((0, 16),), -0.2, 0.2)), 0.2, 5.0),
        "system": gaussian(seeds[1], (SUBSETS, SECTORS, 2, SINO, IMG), IMG ** -0.5, 0.25, ((0, 2), (1, 16)), jnp.float32),
        "pattern": set_ends((jax.random.randint(seeds[2], (SUBSETS, SECTORS, SINO // TILE, IMG // TILE), 0, 4) < 3).astype(jnp.int32), jax.random.fold_in(seeds[2], 1), 0, 1),
        "counts": set_ends(jax.random.randint(seeds[3], (SUBSETS, SECTORS, FRAMES, PLANES, SINO), 0, 16), jax.random.fold_in(seeds[3], 1), 0, 15).astype(jnp.int32),
        "background": jnp.clip(jnp.exp(math.log(4.0) - 1.3862944 * jax.random.uniform(seeds[4], (SUBSETS, SECTORS, FRAMES, PLANES, SINO), jnp.float32) ** level_of(seeds[4], (SUBSETS, SECTORS, FRAMES, PLANES, SINO), ((0, 2), (1, 16)), -0.2, 0.2)), 1.0, 4.0),
        "sensitivity": jnp.clip(jnp.exp(math.log(4.0) - 2.0794415 * jax.random.uniform(seeds[5], (SECTORS, PLANES, IMG), jnp.float32) ** level_of(seeds[5], (SECTORS, PLANES, IMG), ((0, 16), (1, 2)), -0.2, 0.2)), 0.5, 4.0),
    }


def contract_fwd(operator, operand):
    return jnp.einsum("kij,kcj->kci", operator, operand, precision=lax.Precision.HIGHEST)


def contract_back(operator, operand):
    return jnp.einsum("kij,kci->kcj", operator, operand, precision=lax.Precision.HIGHEST)


def reference(activity, system, pattern, counts, background, sensitivity):
    sectors = activity.shape[0]
    columns = FRAMES * PLANES
    flat = activity.reshape(sectors, columns, IMG)
    spectrum = jnp.fft.fft(flat, axis=0)
    real_img = jnp.real(spectrum).astype(jnp.float32)
    imag_img = jnp.imag(spectrum).astype(jnp.float32)
    spread = jnp.repeat(jnp.repeat(pattern.astype(jnp.float32), TILE, axis=2), TILE, axis=3)
    total = jnp.zeros((sectors, columns, IMG), jnp.float32)
    for subset in range(N_SEG):
        matrix = system[subset] * spread[subset][:, None]
        real_sys = matrix[:, 0]
        imag_sys = matrix[:, 1]
        real_fwd = contract_fwd(real_sys, real_img) - contract_fwd(imag_sys, imag_img)
        imag_fwd = contract_fwd(real_sys, imag_img) + contract_fwd(imag_sys, real_img)
        estimate = jnp.real(jnp.fft.ifft(real_fwd + 1j * imag_fwd, axis=0)).astype(jnp.float32)
        expected = jnp.maximum(estimate + background[subset].reshape(sectors, columns, SINO), 1.0)
        quotient = counts[subset].astype(jnp.float32).reshape(sectors, columns, SINO) / expected
        ratio_spec = jnp.fft.fft(quotient, axis=0) / sectors
        real_ratio = jnp.real(ratio_spec).astype(jnp.float32)
        imag_ratio = jnp.imag(ratio_spec).astype(jnp.float32)
        real_back = contract_back(real_sys, real_ratio) + contract_back(imag_sys, imag_ratio)
        imag_back = contract_back(real_sys, imag_ratio) - contract_back(imag_sys, real_ratio)
        summed = jnp.real(jnp.fft.ifft(real_back + 1j * imag_back, axis=0)) * sectors
        total = total + summed.astype(jnp.float32)
    return activity * total.reshape(sectors, FRAMES, PLANES, IMG) / sensitivity[:, None]
```

```python
import functools

import jax
import jax.numpy as jnp
import numpy as np
from jax import lax
from jax.experimental import pallas as pl
from jax.experimental.pallas import tpu as pltpu
from jax.sharding import PartitionSpec as P

BOTH = ("freq", "seg")
precise = lax.Precision.HIGHEST


def analyse(load, start, step, size):
    if size == 1:
        return [(load(start), None)]
    if size == 2:
        first, second = load(start), load(start + step)
        return [(first + second, None), (first - second, None)]
    even = analyse(load, start, 2 * step, size // 2)
    odd = analyse(load, start + step, 2 * step, size // 2)
    half, quarter = size // 2, size // 4
    out = [None] * (half + 1)
    out[0] = (even[0][0] + odd[0][0], None)
    out[half] = (even[0][0] - odd[0][0], None)
    out[quarter] = (even[quarter][0], -odd[quarter][0])
    for k in range(1, quarter):
        cosine, sine = float(np.cos(2 * np.pi * k / size)), float(np.sin(2 * np.pi * k / size))
        real, imag = odd[k]
        turned_real = real * cosine + imag * sine
        turned_imag = imag * cosine - real * sine
        out[k] = (even[k][0] + turned_real, even[k][1] + turned_imag)
        out[half - k] = (even[k][0] - turned_real, turned_imag - even[k][1])
    return out


def synthesise(values, emit, start, step, size):
    if size == 1:
        emit(start, values[0][0])
        return
    if size == 2:
        emit(start, values[0][0] + values[1][0])
        emit(start + step, values[0][0] - values[1][0])
        return
    half, quarter = size // 2, size // 4
    even, odd = [None] * (quarter + 1), [None] * (quarter + 1)
    even[0] = (values[0][0] + values[half][0], None)
    odd[0] = (values[0][0] - values[half][0], None)
    even[quarter] = (values[quarter][0], None)
    odd[quarter] = (-values[quarter][1], None)
    for k in range(1, quarter):
        cosine, sine = float(np.cos(2 * np.pi * k / size)), float(np.sin(2 * np.pi * k / size))
        (real, imag), (other_real, other_imag) = values[k], values[half - k]
        even[k] = (real + other_real, imag - other_imag)
        diff_real, diff_imag = real - other_real, imag + other_imag
        odd[k] = (diff_real * cosine - diff_imag * sine, diff_real * sine + diff_imag * cosine)
    synthesise(even, emit, start, 2 * step, half)
    synthesise(odd, emit, start + step, 2 * step, half)


def analysis_matrix(size):
    angles = 2 * np.pi * np.outer(np.arange(size // 2), np.arange(size)) / size
    table = np.stack([np.cos(angles), -np.sin(angles)], axis=1).reshape(size, size)
    table[1] = np.where(np.arange(size) % 2 == 0, 1.0, -1.0)
    return jnp.asarray(table, jnp.float32)


def load_slots(ref, lanes, size):
    half = size // 2
    values = [(ref[2 * k, 0, :, lanes], ref[2 * k + 1, 0, :, lanes]) for k in range(half)]
    return [(values[0][0], None)] + values[1:] + [(values[0][1], None)]


def store_slots(ref, lanes, spectrum):
    half = len(spectrum) - 1
    ref[0, 0, :, lanes] = spectrum[0][0]
    ref[1, 0, :, lanes] = spectrum[half][0]
    for k in range(1, half):
        ref[2 * k, 0, :, lanes] = spectrum[k][0]
        ref[2 * k + 1, 0, :, lanes] = spectrum[k][1]


def each_lane_tile(width, body):
    def step(index, carry):
        body(pl.ds(pl.multiple_of(index * 128, 128), 128))
        return carry

    lax.fori_loop(0, width // 128, step, 0)


def sector_block(shape):
    hosts, _, local, _, width = shape
    return pl.BlockSpec((hosts, 1, local, 8, width), lambda c, t: (0, c, 0, t, 0))


def slot_block(shape):
    count, _, _, width = shape
    return pl.BlockSpec((count, 1, 8, width), lambda c, t: (0, c, t, 0))


def tile_params():
    return pltpu.CompilerParams(dimension_semantics=("arbitrary", "arbitrary"))


def cost(flops, nbytes):
    return pl.CostEstimate(flops=int(flops), bytes_accessed=int(nbytes), transcendentals=0)


def spectrum_of(section):
    hosts, parts, local, depth, width = section.shape
    count = hosts * local
    if depth % 8 or width % 128:
        flat = section.transpose(0, 2, 1, 3, 4).reshape(count, parts, depth, width)
        return jnp.einsum("us,scpj->ucpj", analysis_matrix(count), flat, precision=precise)

    def kernel(in_ref, out_ref):
        def body(lanes):
            load = lambda s: in_ref[s // local, 0, s % local, :, lanes]
            store_slots(out_ref, lanes, analyse(load, 0, 1, count))

        each_lane_tile(width, body)

    shape = (count, parts, depth, width)
    return pl.pallas_call(
        kernel,
        grid=(parts, depth // 8),
        in_specs=[sector_block(section.shape)],
        out_specs=slot_block(shape),
        out_shape=jax.ShapeDtypeStruct(shape, jnp.float32),
        compiler_params=tile_params(),
        cost_estimate=cost(section.size * 16, section.size * 8),
        name="spectrum",
    )(section)


def sectors_of(spectrum, hosts):
    count, parts, depth, width = spectrum.shape
    local = count // hosts
    shape = (hosts, parts, local, depth, width)
    if depth % 8 or width % 128:
        flat = jnp.einsum("us,ucpj->scpj", analysis_matrix(count), spectrum, precision=precise)
        return flat.reshape(hosts, local, parts, depth, width).transpose(0, 2, 1, 3, 4)

    def kernel(in_ref, out_ref):
        def body(lanes):
            def emit(s, value):
                out_ref[s // local, 0, s % local, :, lanes] = value

            synthesise(load_slots(in_ref, lanes, count), emit, 0, 1, count)

        each_lane_tile(width, body)

    return pl.pallas_call(
        kernel,
        grid=(parts, depth // 8),
        in_specs=[slot_block(spectrum.shape)],
        out_specs=sector_block(shape),
        out_shape=jax.ShapeDtypeStruct(shape, jnp.float32),
        compiler_params=tile_params(),
        cost_estimate=cost(spectrum.size * 16, spectrum.size * 8),
        name="sectors",
    )(spectrum)


def ratio_of(forward, counts, background):
    count, parts, depth, width = forward.shape
    hosts, _, local = counts.shape[:3]
    scale = 1.0 / count
    if depth % 8 or width % 128:
        estimate = sectors_of(forward, hosts) * scale
        expected = jnp.maximum(estimate + background, 1.0)
        return spectrum_of(counts.astype(jnp.float32) / expected * scale)

    def kernel(in_ref, counts_ref, ground_ref, out_ref, held):
        def body(lanes):
            def emit(s, value):
                at = (s // local, 0, s % local, slice(None), lanes)
                expected = jnp.maximum(value * scale + ground_ref[at], 1.0)
                held[s] = counts_ref[at].astype(jnp.float32) / expected * scale

            synthesise(load_slots(in_ref, lanes, count), emit, 0, 1, count)
            store_slots(out_ref, lanes, analyse(lambda s: held[s], 0, 1, count))

        each_lane_tile(width, body)

    return pl.pallas_call(
        kernel,
        grid=(parts, depth // 8),
        in_specs=[slot_block(forward.shape), sector_block(counts.shape), sector_block(counts.shape)],
        out_specs=slot_block(forward.shape),
        out_shape=jax.ShapeDtypeStruct(forward.shape, jnp.float32),
        scratch_shapes=[pltpu.VMEM((count, 8, 128), jnp.float32)],
        compiler_params=tile_params(),
        cost_estimate=cost(forward.size * 48, forward.size * 16),
        name="ratio",
    )(forward, counts, background)


def masked_block(system, pattern, which):
    _, local, _, height, width = system.shape
    rows, cols = pattern.shape[2:]
    tile_height, tile_width = height // rows, width // cols

    def kernel(which_ref, pattern_ref, in_ref, out_ref):
        row = pl.program_id(1)
        for col in range(cols):
            lanes = slice(col * tile_width, (col + 1) * tile_width)
            value = pattern_ref[(which_ref[0] * rows + row) * cols + col].astype(jnp.float32)
            out_ref[0, :, lanes] = in_ref[0, 0, 0, :, lanes] * value

    return pl.pallas_call(
        kernel,
        grid_spec=pltpu.PrefetchScalarGridSpec(
            num_scalar_prefetch=2,
            grid=(2, rows),
            in_specs=[pl.BlockSpec((1, 1, 1, tile_height, width), lambda a, t, w, _: (0, w[0], a, t, 0))],
            out_specs=pl.BlockSpec((1, tile_height, width), lambda a, t, w, _: (a, t, 0)),
        ),
        out_shape=jax.ShapeDtypeStruct((2, height, width), jnp.float32),
        cost_estimate=cost(2 * height * width, 16 * height * width),
        compiler_params=tile_params(),
        name="masked",
    )(which.reshape(1), pattern.reshape(-1), system)


def split(value):
    high = value.astype(jnp.bfloat16)
    return high, (value - high.astype(jnp.float32)).astype(jnp.bfloat16)


def operator_of(first, second, weights, slot):
    keep, sign = weights[slot, 0], weights[slot, 1]
    return first[0] + keep * second[0], keep * first[0] + second[0], sign * (first[1] - second[1])


def apply_blocks(blocks, weights, spectra, adjoint):
    hosts, reals, parts, depth, width = spectra.shape
    slots = reals // 2
    height, inner = blocks[0].shape[1:]
    result = height if not adjoint else inner
    if depth % 8 or width % 128 or result % 128:
        outs = []
        for slot in range(slots):
            upper, lower, cross = operator_of(blocks[2 * slot], blocks[2 * slot + 1], weights, slot)
            real, imag = spectra[:, 2 * slot], spectra[:, 2 * slot + 1]
            form = "ncpi,ij->ncpj" if adjoint else "ncpj,ij->ncpi"
            dot = functools.partial(jnp.einsum, form, precision=precise)
            flip = -1.0 if adjoint else 1.0
            outs.append(dot(real, upper) - flip * dot(imag, cross))
            outs.append(dot(imag, lower) + flip * dot(real, cross))
        return jnp.stack(outs, axis=1)

    group = hosts
    while group * parts * depth > 256 and group % 2 == 0:
        group //= 2
    rows = group * parts * depth
    chunk = 128 if height % 128 == 0 else height
    panel = 256 if result % 256 == 0 else 128

    def kernel(weights_ref, *refs):
        raw, in_ref, out_ref = refs[: 2 * slots], refs[2 * slots], refs[2 * slots + 1]
        high_ref, low_ref, lhs_high, lhs_low = refs[2 * slots + 2 :]

        def put(slot, at, value):
            high, low = split(value)
            high_ref[(slot,) + at] = high
            low_ref[(slot,) + at] = low

        @pl.when(pl.program_id(0) == 0)
        def _():
            for slot in range(slots):

                def fold(index, carry, slot=slot):
                    at = pl.ds(pl.multiple_of(index * chunk, chunk), chunk)
                    at2 = pl.ds(pl.multiple_of(index * chunk + height, chunk), chunk)
                    first = [raw[2 * slot][part, at, :] for part in range(2)]
                    second = [raw[2 * slot + 1][part, at, :] for part in range(2)]
                    upper, lower, cross = operator_of(first, second, weights_ref, slot)
                    one, two = slice(0, inner), slice(inner, 2 * inner)
                    if adjoint:
                        put(slot, (at, one), upper)
                        put(slot, (at, two), -cross)
                        put(slot, (at2, one), cross)
                        put(slot, (at2, two), lower)
                    else:
                        cross = cross.T
                        put(slot, (one, at), upper.T)
                        put(slot, (one, at2), cross)
                        put(slot, (two, at), -cross)
                        put(slot, (two, at2), lower.T)
                    return carry

                lax.fori_loop(0, height // chunk, fold, 0)

        for slot in range(slots):
            for part in range(2):
                lanes = slice(part * width, (part + 1) * width)
                high, low = split(in_ref[:, 2 * slot + part].reshape(rows, width))
                lhs_high[slot, :, lanes] = high
                lhs_low[slot, :, lanes] = low
        per_part = result // panel

        def multiply(index, carry):
            at = pl.ds(pl.multiple_of(index * panel, panel), panel)
            out_at = pl.ds(pl.multiple_of(index % per_part * panel, panel), panel)
            for slot in range(slots):
                dot = functools.partial(jnp.dot, preferred_element_type=jnp.float32)
                right_high, right_low = high_ref[slot, :, at], low_ref[slot, :, at]
                total = dot(lhs_high[slot], right_low) + dot(lhs_low[slot], right_high)
                total = total + dot(lhs_high[slot], right_high)
                shape = (group, parts, depth, panel)
                out_ref[:, 2 * slot + index // per_part, :, :, out_at] = total.reshape(shape)
            return carry

        lax.fori_loop(0, 2 * per_part, multiply, 0)

    def block(last):
        return pl.BlockSpec((group, reals, parts, depth, last), lambda t, w: (t, 0, 0, 0, 0))

    whole = pl.BlockSpec((2, height, inner), lambda t, w: (0, 0, 0), pipeline_mode=pl.Buffered(1))
    shape = (hosts, reals, parts, depth, result)
    return pl.pallas_call(
        kernel,
        grid_spec=pltpu.PrefetchScalarGridSpec(
            num_scalar_prefetch=1,
            grid=(hosts // group,),
            in_specs=[whole] * (2 * slots) + [block(width)],
            out_specs=block(result),
            scratch_shapes=[pltpu.VMEM((slots, 2 * width, 2 * result), jnp.bfloat16)] * 2
            + [pltpu.VMEM((slots, rows, 2 * width), jnp.bfloat16)] * 2,
        ),
        out_shape=jax.ShapeDtypeStruct(shape, jnp.float32),
        compiler_params=pltpu.CompilerParams(dimension_semantics=("arbitrary",)),
        cost_estimate=cost(24 * slots * hosts * parts * depth * width * result, 3 * 2**23),
        name="adjoint" if adjoint else "project",
    )(weights, *blocks, spectra)


def routes(count, hosts, parts):
    local, slots = count // hosts, count // 2 // hosts
    rounds = []
    for slot in range(slots):
        for turn in range(2):
            sent, pairs = [None] * hosts, []
            for i in range(hosts):
                k = slots * i + slot
                if (i + turn) % 2:
                    k = count - k if k else count // 2
                source = k // local
                assert sent[source] is None
                sent[source] = k % local
                pairs += [(source * parts + g, g * hosts + i) for g in range(parts)]
            rounds.append((sent, pairs))
    return rounds


def on_device(hosts, parts, activity, system, pattern, counts, background, sensitivity):
    local, frames, planes, image = activity.shape
    sino = system.shape[3]
    count = local * hosts
    slots = count // 2 // hosts
    share = planes // parts
    depth = frames * share // hosts
    device = lax.axis_index(BOTH)
    freq, seg = lax.axis_index("freq"), lax.axis_index("seg")
    place = device % hosts
    sides = [[g * hosts + i for i in range(hosts)] for g in range(parts)]

    def exchange_all(array):
        return lax.all_to_all(array, BOTH, split_axis=0, concat_axis=0, tiled=True)

    def exchange_side(array):
        return lax.all_to_all(
            array, BOTH, split_axis=0, concat_axis=0, tiled=True, axis_index_groups=sides
        )

    current = lax.dynamic_slice_in_dim(activity, seg * share, share, 2)
    chunks = current.reshape(local, hosts, depth, image).transpose(1, 0, 2, 3)
    chunks = jnp.broadcast_to(chunks[None], (parts,) + chunks.shape)
    columns = exchange_all(chunks.reshape(parts * hosts, local, depth, image))
    columns = columns.reshape(hosts, parts, local, depth, image)

    tables = routes(count, hosts, parts)
    masked = [masked_block(system, pattern, jnp.asarray(sent, jnp.int32)[freq]) for sent, _ in tables]
    columns, masked = lax.optimization_barrier((columns, masked))
    blocks = [lax.ppermute(block, BOTH, pairs) for block, (_, pairs) in zip(masked, tables)]
    keep = jnp.where(slots * place + jnp.arange(slots) == 0, 0.0, 1.0)
    sign = keep * jnp.where(place % 2 == 0, 1.0, -1.0)
    weights = jnp.stack([keep, sign], axis=1)

    def to_side(array):
        array = array[0].reshape(local, frames, parts, share, sino).transpose(2, 0, 1, 3, 4)
        array = array.reshape(parts, local, hosts, depth, sino).transpose(0, 2, 1, 3, 4)
        return lax.all_to_all(array, "seg", split_axis=0, concat_axis=0, tiled=True)

    def to_columns(array):
        array = exchange_all(array.reshape(parts * hosts, local, depth, sino))
        return array.reshape(hosts, parts, local, depth, sino)

    staged = (to_side(counts), to_side(background))
    blocks, staged = lax.optimization_barrier((blocks, staged))
    counts_cols, ground_cols = [to_columns(array) for array in staged]

    def by_owner(array):
        return array.reshape(hosts, 2 * slots, parts, depth, array.shape[-1])

    def by_slot(array):
        return array.reshape(count, parts, depth, array.shape[-1])

    spectra = exchange_side(by_owner(spectrum_of(columns)))
    forward = exchange_side(apply_blocks(blocks, weights, spectra, False))
    ratio = ratio_of(by_slot(forward), counts_cols, ground_cols)
    spectra = exchange_side(by_owner(ratio))
    backward = exchange_side(apply_blocks(blocks, weights, spectra, True))
    back = sectors_of(by_slot(backward), hosts)
    back = exchange_all(back.reshape(hosts * parts, local, depth, image))
    total = back.reshape(parts, hosts, local, depth, image).sum(0).transpose(1, 0, 2, 3)
    total = total.reshape(local, frames, share, image)
    return current * total / sensitivity[:, None]


def solution(mesh):
    in_specs = (
        P("freq", None, None, None),
        P("seg", "freq", None, None, None),
        P("seg", "freq", None, None),
        P("seg", "freq", None, None, None),
        P("seg", "freq", None, None, None),
        P("freq", "seg", None),
    )
    body = functools.partial(on_device, mesh.shape["freq"], mesh.shape["seg"])
    return jax.shard_map(
        body, mesh=mesh, in_specs=in_specs, out_specs=P("freq", None, "seg", None), check_vma=False
    )
```

```python
import functools

import jax
import jax.numpy as jnp
import numpy as np
from jax import lax
from jax.experimental import pallas as pl
from jax.experimental.pallas import tpu as pltpu
from jax.sharding import PartitionSpec as P

BOTH = ("freq", "seg")
precise = lax.Precision.HIGHEST


def analyse(load, start, step, size):
    if size == 1:
        return [(load(start), None)]
    if size == 2:
        first, second = load(start), load(start + step)
        return [(first + second, None), (first - second, None)]
    even = analyse(load, start, 2 * step, size // 2)
    odd = analyse(load, start + step, 2 * step, size // 2)
    half, quarter = size // 2, size // 4
    out = [None] * (half + 1)
    out[0] = (even[0][0] + odd[0][0], None)
    out[half] = (even[0][0] - odd[0][0], None)
    out[quarter] = (even[quarter][0], -odd[quarter][0])
    for k in range(1, quarter):
        cosine, sine = float(np.cos(2 * np.pi * k / size)), float(np.sin(2 * np.pi * k / size))
        real, imag = odd[k]
        turned_real = real * cosine + imag * sine
        turned_imag = imag * cosine - real * sine
        out[k] = (even[k][0] + turned_real, even[k][1] + turned_imag)
        out[half - k] = (even[k][0] - turned_real, turned_imag - even[k][1])
    return out


def synthesise(values, emit, start, step, size):
    if size == 1:
        emit(start, values[0][0])
        return
    if size == 2:
        emit(start, values[0][0] + values[1][0])
        emit(start + step, values[0][0] - values[1][0])
        return
    half, quarter = size // 2, size // 4
    even, odd = [None] * (quarter + 1), [None] * (quarter + 1)
    even[0] = (values[0][0] + values[half][0], None)
    odd[0] = (values[0][0] - values[half][0], None)
    even[quarter] = (values[quarter][0], None)
    odd[quarter] = (-values[quarter][1], None)
    for k in range(1, quarter):
        cosine, sine = float(np.cos(2 * np.pi * k / size)), float(np.sin(2 * np.pi * k / size))
        (real, imag), (other_real, other_imag) = values[k], values[half - k]
        even[k] = (real + other_real, imag - other_imag)
        diff_real, diff_imag = real - other_real, imag + other_imag
        odd[k] = (diff_real * cosine - diff_imag * sine, diff_real * sine + diff_imag * cosine)
    synthesise(even, emit, start, 2 * step, half)
    synthesise(odd, emit, start + step, 2 * step, half)


def analysis_matrix(size):
    angles = 2 * np.pi * np.outer(np.arange(size // 2), np.arange(size)) / size
    table = np.stack([np.cos(angles), -np.sin(angles)], axis=1).reshape(size, size)
    table[1] = np.where(np.arange(size) % 2 == 0, 1.0, -1.0)
    return jnp.asarray(table, jnp.float32)


def load_slots(ref, lanes, size):
    half = size // 2
    values = [(ref[2 * k, 0, :, lanes], ref[2 * k + 1, 0, :, lanes]) for k in range(half)]
    return [(values[0][0], None)] + values[1:] + [(values[0][1], None)]


def store_slots(ref, lanes, spectrum):
    half = len(spectrum) - 1
    ref[0, 0, :, lanes] = spectrum[0][0]
    ref[1, 0, :, lanes] = spectrum[half][0]
    for k in range(1, half):
        ref[2 * k, 0, :, lanes] = spectrum[k][0]
        ref[2 * k + 1, 0, :, lanes] = spectrum[k][1]


def each_lane_tile(width, body):
    def step(index, carry):
        body(pl.ds(pl.multiple_of(index * 128, 128), 128))
        return carry

    lax.fori_loop(0, width // 128, step, 0)


def tile_params(axes):
    return pltpu.CompilerParams(dimension_semantics=("arbitrary",) * axes)


def cost(flops, nbytes):
    return pl.CostEstimate(flops=int(flops), bytes_accessed=int(nbytes), transcendentals=0)


def slot_block(shape, part=None):
    count, _, _, width = shape
    if part is None:
        return pl.BlockSpec((count, 1, 8, width), lambda c, t: (0, c, t, 0))
    return pl.BlockSpec((count, 1, 8, width), lambda t: (0, part, t, 0))


def spectrum_of(section):
    hosts, parts, local, depth, width = section.shape
    count = hosts * local
    if depth % 8 or width % 128:
        flat = section.transpose(0, 2, 1, 3, 4).reshape(count, parts, depth, width)
        return jnp.einsum("us,scpj->ucpj", analysis_matrix(count), flat, precision=precise)

    def kernel(in_ref, out_ref):
        def body(lanes):
            load = lambda s: in_ref[s // local, 0, s % local, :, lanes]
            store_slots(out_ref, lanes, analyse(load, 0, 1, count))

        each_lane_tile(width, body)

    shape = (count, parts, depth, width)
    return pl.pallas_call(
        kernel,
        grid=(parts, depth // 8),
        in_specs=[pl.BlockSpec((hosts, 1, local, 8, width), lambda c, t: (0, c, 0, t, 0))],
        out_specs=slot_block(shape),
        out_shape=jax.ShapeDtypeStruct(shape, jnp.float32),
        compiler_params=tile_params(2),
        cost_estimate=cost(section.size * 16, section.size * 8),
        name="spectrum",
    )(section)


def place_of(s, local, hosts, sides):
    host, within = s // local, hosts // sides
    return host % within * sides + host // within, s % local


def sectors_of(spectrum, hosts, sides):
    count, _, depth, width = spectrum.shape
    local = count // hosts
    shape = (hosts, local, depth, width)
    if depth % 8 or width % 128:
        flat = jnp.einsum("us,ucpj->scpj", analysis_matrix(count), spectrum, precision=precise)
        flat = flat.reshape(sides, hosts // sides, local, depth, width)
        return flat.transpose(1, 0, 2, 3, 4).reshape(shape)

    def kernel(in_ref, out_ref):
        def body(lanes):
            def emit(s, value):
                host, row = place_of(s, local, hosts, sides)
                out_ref[host, row, :, lanes] = value

            synthesise(load_slots(in_ref, lanes, count), emit, 0, 1, count)

        each_lane_tile(width, body)

    return pl.pallas_call(
        kernel,
        grid=(depth // 8,),
        in_specs=[slot_block(spectrum.shape, 0)],
        out_specs=pl.BlockSpec((hosts, local, 8, width), lambda t: (0, 0, t, 0)),
        out_shape=jax.ShapeDtypeStruct(shape, jnp.float32),
        compiler_params=tile_params(1),
        cost_estimate=cost(spectrum.size * 16, spectrum.size * 8),
        name="sectors",
    )(spectrum)


def ratio_of(forward, measured, part, sides):
    count, _, depth, width = forward.shape
    hosts, _, local = measured.shape[:3]
    scale = 1.0 / count
    shape = (count, 1, depth, width)
    if depth % 8 or width % 128:
        flat = forward[:, part : part + 1]
        estimate = sectors_of(flat, hosts, sides) * scale
        expected = jnp.maximum(estimate + measured[:, 1], 1.0)
        quotient = (measured[:, 0] / expected * scale).reshape(hosts // sides, sides, local, depth, width)
        quotient = quotient.transpose(1, 0, 2, 3, 4).reshape(hosts, 1, local, depth, width)
        return spectrum_of(quotient)

    def kernel(in_ref, measured_ref, out_ref, held):
        def body(lanes):
            def emit(s, value):
                host, row = place_of(s, local, hosts, sides)
                expected = jnp.maximum(value * scale + measured_ref[host, 1, row, :, lanes], 1.0)
                held[s] = measured_ref[host, 0, row, :, lanes] / expected * scale

            synthesise(load_slots(in_ref, lanes, count), emit, 0, 1, count)
            store_slots(out_ref, lanes, analyse(lambda s: held[s], 0, 1, count))

        each_lane_tile(width, body)

    return pl.pallas_call(
        kernel,
        grid=(depth // 8,),
        in_specs=[
            slot_block(forward.shape, part),
            pl.BlockSpec((hosts, 2, local, 8, width), lambda t: (0, 0, 0, t, 0)),
        ],
        out_specs=slot_block(shape, 0),
        out_shape=jax.ShapeDtypeStruct(shape, jnp.float32),
        scratch_shapes=[pltpu.VMEM((count, 8, 128), jnp.float32)],
        compiler_params=tile_params(1),
        cost_estimate=cost(measured.size * 24, measured.size * 8),
        name="ratio",
    )(forward, measured)


def masked_block(system, pattern, which):
    _, local, _, height, width = system.shape
    rows, cols = pattern.shape[2:]
    tile_height, tile_width = height // rows, width // cols

    def kernel(which_ref, pattern_ref, in_ref, out_ref):
        for row in range(rows):
            for col in range(cols):
                at = (slice(row * tile_height, (row + 1) * tile_height),)
                at += (slice(col * tile_width, (col + 1) * tile_width),)
                value = pattern_ref[(which_ref[0] * rows + row) * cols + col].astype(jnp.float32)
                out_ref[(0,) + at] = in_ref[(0, 0, 0) + at] * value

    return pl.pallas_call(
        kernel,
        grid_spec=pltpu.PrefetchScalarGridSpec(
            num_scalar_prefetch=2,
            grid=(2,),
            in_specs=[pl.BlockSpec((1, 1, 1, height, width), lambda a, w, _: (0, w[0], a, 0, 0))],
            out_specs=pl.BlockSpec((1, height, width), lambda a, w, _: (a, 0, 0)),
        ),
        out_shape=jax.ShapeDtypeStruct((2, height, width), jnp.float32),
        cost_estimate=cost(2 * height * width, 16 * height * width),
        compiler_params=tile_params(1),
        name="masked",
    )(which.reshape(1), pattern.reshape(-1), system)


def split(value):
    high = value.astype(jnp.bfloat16)
    return high, (value - high.astype(jnp.float32)).astype(jnp.bfloat16)


def folded(first, second, weights):
    own, other, sign = weights[0], weights[1], weights[2]
    upper = own * first[0] + other * second[0]
    lower = other * first[0] + own * second[0]
    return upper, lower, sign * (first[1] - second[1])


def operator_of(first, second, weights, adjoint):
    height, inner = first.shape[1:]
    if height % 128 or inner % 128:
        upper, lower, cross = folded(first, second, weights)
        if adjoint:
            table = jnp.block([[upper, -cross], [cross, lower]])
        else:
            table = jnp.block([[upper.T, cross.T], [-cross.T, lower.T]])
        return split(table)
    shape = (2 * height, 2 * inner) if adjoint else (2 * inner, 2 * height)

    def kernel(weights_ref, first_ref, second_ref, high_ref, low_ref):
        def put(at, value):
            high_ref[at], low_ref[at] = split(value)

        index = pl.program_id(0)
        at = pl.ds(pl.multiple_of(index * 128, 128), 128)
        at2 = pl.ds(pl.multiple_of(index * 128 + height, 128), 128)
        upper, lower, cross = folded(first_ref, second_ref, weights_ref)
        one, two = slice(0, inner), slice(inner, 2 * inner)
        if adjoint:
            put((at, one), upper)
            put((at, two), -cross)
            put((at2, one), cross)
            put((at2, two), lower)
        else:
            cross = cross.T
            put((one, at), upper.T)
            put((one, at2), cross)
            put((two, at), -cross)
            put((two, at2), lower.T)

    return pl.pallas_call(
        kernel,
        grid_spec=pltpu.PrefetchScalarGridSpec(
            num_scalar_prefetch=1,
            grid=(height // 128,),
            in_specs=[pl.BlockSpec((2, 128, inner), lambda t, w: (0, t, 0))] * 2,
            out_specs=[pl.BlockSpec(shape, lambda t, w: (0, 0))] * 2,
        ),
        out_shape=[jax.ShapeDtypeStruct(shape, jnp.bfloat16)] * 2,
        compiler_params=tile_params(1),
        cost_estimate=cost(16 * height * inner, 32 * height * inner),
        name="operator",
    )(weights, first, second)


def apply_operators(operators, spectra, name):
    hosts, reals, parts, depth, width = spectra.shape
    slots = reals // 2
    result = operators[0][0].shape[1] // 2
    if depth % 8 or width % 128 or result % 256:
        outs = []
        for slot, (high, low) in enumerate(operators):
            table = high.astype(jnp.float32) + low.astype(jnp.float32)
            rows = jnp.concatenate([spectra[:, 2 * slot], spectra[:, 2 * slot + 1]], axis=-1)
            out = jnp.einsum("ncpi,ij->ncpj", rows, table, precision=precise)
            outs += [out[..., :result], out[..., result:]]
        return jnp.stack(outs, axis=1)

    panel, per_part = 256, result // 256
    group = hosts
    while group * parts * depth > 256 and group % 2 == 0:
        group //= 2
    rows = group * parts * depth

    def kernel(*refs):
        terms, in_ref, out_ref, lhs_high, lhs_low = refs[: 2 * slots], *refs[2 * slots :]

        @pl.when(pl.program_id(0) == 0)
        def _():
            for slot in range(slots):
                for part in range(2):
                    lanes = slice(part * width, (part + 1) * width)
                    value = in_ref[:, 2 * slot + part].reshape(hosts * parts * depth, width)
                    lhs_high[slot, :, lanes], lhs_low[slot, :, lanes] = split(value)

        dot = functools.partial(jnp.dot, preferred_element_type=jnp.float32)

        def multiply(index, carry):
            at = pl.ds(pl.multiple_of(index * rows, rows), rows)
            out_at = pl.ds(index * group, group)
            for slot in range(slots):
                high, low = terms[2 * slot][...], terms[2 * slot + 1][...]
                total = dot(lhs_high[slot, at, :], low) + dot(lhs_low[slot, at, :], high)
                total = total + dot(lhs_high[slot, at, :], high)
                out_ref[out_at, slot, 0] = total.reshape(group, parts, depth, panel)
            return carry

        lax.fori_loop(0, hosts // group, multiply, 0)

    shape = (hosts, slots, 2, parts, depth, result)
    out = pl.pallas_call(
        kernel,
        grid=(2 * per_part,),
        in_specs=[pl.BlockSpec((2 * width, panel), lambda t: (0, t))] * (2 * slots)
        + [pl.BlockSpec(spectra.shape, lambda t: (0, 0, 0, 0, 0))],
        out_specs=pl.BlockSpec(
            (hosts, slots, 1, parts, depth, panel),
            lambda t: (0, 0, t // per_part, 0, 0, t % per_part),
        ),
        out_shape=jax.ShapeDtypeStruct(shape, jnp.float32),
        scratch_shapes=[pltpu.VMEM((slots, hosts * parts * depth, 2 * width), jnp.bfloat16)] * 2,
        compiler_params=tile_params(1),
        cost_estimate=cost(24 * slots * hosts * parts * depth * width * result, 3 * 2**23),
        name=name,
    )(*[term for pair in operators for term in pair], spectra)
    return out.reshape(hosts, reals, parts, depth, result)


def routes(count, hosts, sides):
    local, slots = count // hosts, count // 2 // hosts
    rounds = []
    for slot in range(slots):
        for turn in range(2):
            sent, direct, inside, across = [None] * (hosts * sides), [], [], []
            for g in range(sides):
                for i in range(hosts):
                    k = slots * i + slot
                    if (i + turn + g) % 2:
                        k = count - k if k else count // 2
                    host = k // local
                    source, middle = host * sides + g, host * sides // hosts * hosts + i
                    assert sent[source] is None
                    sent[source] = k % local
                    direct.append((source, g * hosts + i))
                    inside.append((source, middle))
                    across.append((middle, g * hosts + i))
            two_hops = len({middle for _, middle in inside}) == hosts * sides
            rounds.append((sent, [inside, across] if two_hops else [direct]))
    return rounds


def on_device(hosts, sides, activity, system, pattern, counts, background, sensitivity):
    local, frames, planes, image = activity.shape
    sino = system.shape[3]
    count = local * hosts
    slots = count // 2 // hosts
    share = planes // sides
    depth = frames * share // hosts
    device = lax.axis_index(BOTH)
    seg = lax.axis_index("seg")
    side, place = device // hosts, device % hosts
    groups = [[g * hosts + i for i in range(hosts)] for g in range(sides)]
    within = hosts // sides
    swap = [
        ((a * within + f) * sides + b, (b * within + f) * sides + a)
        for a in range(sides)
        for f in range(within)
        for b in range(sides)
    ]

    def exchange_side(array):
        return lax.all_to_all(
            array, BOTH, split_axis=0, concat_axis=0, tiled=True, axis_index_groups=groups
        )

    current = lax.dynamic_slice_in_dim(activity, seg * share, share, 2)
    chunks = current.reshape(local, hosts, depth, image).transpose(1, 0, 2, 3)
    chunks = jnp.broadcast_to(chunks[None], (sides,) + chunks.shape)
    columns = lax.all_to_all(
        chunks.reshape(sides * hosts, local, depth, image),
        BOTH,
        split_axis=0,
        concat_axis=0,
        tiled=True,
    )
    columns = columns.reshape(hosts, sides, local, depth, image)

    blocks = []
    for sent, hops in routes(count, hosts, sides):
        block = masked_block(system, pattern, jnp.asarray(sent, jnp.int32)[device])
        for pairs in hops[:-1]:
            block = lax.ppermute(block, BOTH, pairs)
        blocks.append((block, hops[-1]))
    moved, columns = lax.optimization_barrier(([block for block, _ in blocks], columns))
    blocks = [lax.ppermute(block, BOTH, pairs) for block, (_, pairs) in zip(moved, blocks)]
    odd = (place + side) % 2
    zero = slots * place + jnp.arange(slots) == 0
    own = jnp.where(zero & (odd == 1), 0.0, 1.0)
    other = jnp.where(zero & (odd == 0), 0.0, 1.0)
    sign = jnp.where(zero, 0.0, 1.0 - 2.0 * odd)
    weights = jnp.stack([own, other, sign], axis=1)

    measured = jnp.stack([counts[0].astype(jnp.float32), background[0]])
    measured = measured.reshape(2, local, frames, sides, share, sino)
    parts = []
    for part in range(sides):
        array = measured[:, :, :, part].reshape(2, local, hosts, depth, sino)
        parts.append(array.transpose(2, 0, 1, 3, 4))
    blocks, parts = lax.optimization_barrier((blocks, parts))
    parts = [lax.ppermute(array, BOTH, swap) for array in parts]
    parts = [exchange_side(array) for array in parts]

    def by_owner(array):
        return array.reshape((hosts, 2 * slots) + array.shape[1:])

    def by_slot(array):
        return array.reshape((count,) + array.shape[2:])

    pairs = [(blocks[2 * slot], blocks[2 * slot + 1], weights[slot]) for slot in range(slots)]
    spectra = exchange_side(by_owner(spectrum_of(columns)))
    project = [operator_of(*pair, False) for pair in pairs]
    forward = by_slot(exchange_side(apply_operators(project, spectra, "project")))
    adjoint = [operator_of(*pair, True) for pair in pairs]
    results = []
    for part in range(sides):
        ratio = ratio_of(forward, parts[part], part, sides)
        spectra = exchange_side(by_owner(ratio))
        backward = by_slot(exchange_side(apply_operators(adjoint, spectra, "adjoint")))
        back = exchange_side(sectors_of(backward, hosts, sides))
        results.append(lax.ppermute(back, BOTH, swap))
    back = lax.all_to_all(jnp.stack(results), "seg", split_axis=0, concat_axis=0, tiled=True)
    total = back.sum(0).transpose(1, 0, 2, 3).reshape(local, frames, share, image)
    return current * total / sensitivity[:, None]


def solution(mesh):
    in_specs = (
        P("freq", None, None, None),
        P("seg", "freq", None, None, None),
        P("seg", "freq", None, None),
        P("seg", "freq", None, None, None),
        P("seg", "freq", None, None, None),
        P("freq", "seg", None),
    )
    body = functools.partial(on_device, mesh.shape["freq"], mesh.shape["seg"])
    return jax.shard_map(
        body, mesh=mesh, in_specs=in_specs, out_specs=P("freq", None, "seg", None), check_vma=False
    )
```

```python
import functools

import jax
import jax.numpy as jnp
import numpy as np
from jax import lax
from jax.experimental import pallas as pl
from jax.experimental.pallas import tpu as pltpu
from jax.sharding import PartitionSpec as P

BOTH = ("freq", "seg")
precise = lax.Precision.HIGHEST


def analyse(load, start, step, size):
    if size == 1:
        return [(load(start), None)]
    if size == 2:
        first, second = load(start), load(start + step)
        return [(first + second, None), (first - second, None)]
    even = analyse(load, start, 2 * step, size // 2)
    odd = analyse(load, start + step, 2 * step, size // 2)
    half, quarter = size // 2, size // 4
    out = [None] * (half + 1)
    out[0] = (even[0][0] + odd[0][0], None)
    out[half] = (even[0][0] - odd[0][0], None)
    out[quarter] = (even[quarter][0], -odd[quarter][0])
    for k in range(1, quarter):
        cosine, sine = float(np.cos(2 * np.pi * k / size)), float(np.sin(2 * np.pi * k / size))
        real, imag = odd[k]
        turned_real = real * cosine + imag * sine
        turned_imag = imag * cosine - real * sine
        out[k] = (even[k][0] + turned_real, even[k][1] + turned_imag)
        out[half - k] = (even[k][0] - turned_real, turned_imag - even[k][1])
    return out


def synthesise(values, emit, start, step, size):
    if size == 1:
        emit(start, values[0][0])
        return
    if size == 2:
        emit(start, values[0][0] + values[1][0])
        emit(start + step, values[0][0] - values[1][0])
        return
    half, quarter = size // 2, size // 4
    even, odd = [None] * (quarter + 1), [None] * (quarter + 1)
    even[0] = (values[0][0] + values[half][0], None)
    odd[0] = (values[0][0] - values[half][0], None)
    even[quarter] = (values[quarter][0], None)
    odd[quarter] = (-values[quarter][1], None)
    for k in range(1, quarter):
        cosine, sine = float(np.cos(2 * np.pi * k / size)), float(np.sin(2 * np.pi * k / size))
        (real, imag), (other_real, other_imag) = values[k], values[half - k]
        even[k] = (real + other_real, imag - other_imag)
        diff_real, diff_imag = real - other_real, imag + other_imag
        odd[k] = (diff_real * cosine - diff_imag * sine, diff_real * sine + diff_imag * cosine)
    synthesise(even, emit, start, 2 * step, half)
    synthesise(odd, emit, start + step, 2 * step, half)


def analysis_matrix(size):
    angles = 2 * np.pi * np.outer(np.arange(size // 2), np.arange(size)) / size
    table = np.stack([np.cos(angles), -np.sin(angles)], axis=1).reshape(size, size)
    table[1] = np.where(np.arange(size) % 2 == 0, 1.0, -1.0)
    return jnp.asarray(table, jnp.float32)


def slot_index(k, half, flip):
    return k + flip * ((half - k) % half - k)


def load_slots(ref, lanes, size, flip):
    half = size // 2
    at = [2 * slot_index(k, half, flip) for k in range(half)]
    values = [(ref[row, 0, :, lanes], ref[row + 1, 0, :, lanes]) for row in at]
    return [(values[0][0], None)] + values[1:] + [(values[0][1], None)]


def store_slots(ref, lanes, spectrum, flip):
    half = len(spectrum) - 1
    ref[0, 0, :, lanes] = spectrum[0][0]
    ref[1, 0, :, lanes] = spectrum[half][0]
    for k in range(1, half):
        row = 2 * slot_index(k, half, flip)
        ref[row, 0, :, lanes] = spectrum[k][0]
        ref[row + 1, 0, :, lanes] = spectrum[k][1]


def flipped_matrix(size, flip):
    table = analysis_matrix(size).reshape(size // 2, 2, size)
    order = slot_index(np.arange(size // 2), size // 2, flip)
    return table[order].reshape(size, size)


def each_lane_tile(width, body):
    def step(index, carry):
        body(pl.ds(pl.multiple_of(index * 128, 128), 128))
        return carry

    lax.fori_loop(0, width // 128, step, 0)


def tile_params(axes):
    return pltpu.CompilerParams(dimension_semantics=("arbitrary",) * axes)


def cost(flops, nbytes):
    return pl.CostEstimate(flops=int(flops), bytes_accessed=int(nbytes), transcendentals=0)


def slot_block(shape, part=0):
    count, _, _, width = shape
    return pl.BlockSpec((count, 1, 8, width), lambda t, _: (0, part, t, 0))


def place_of(s, local, hosts, sides):
    host, within = s // local, hosts // sides
    return host % within * sides + host // within, s % local


def tiles_call(kernel, flip, operands, in_specs, shape, out_spec, scratch=()):
    steps = operands[0].shape[-2] // 8
    size = sum(operand.size for operand in operands)
    return pl.pallas_call(
        kernel,
        grid_spec=pltpu.PrefetchScalarGridSpec(
            num_scalar_prefetch=1,
            grid=(steps,),
            in_specs=in_specs,
            out_specs=out_spec,
            scratch_shapes=scratch,
        ),
        out_shape=jax.ShapeDtypeStruct(shape, jnp.float32),
        compiler_params=tile_params(1),
        cost_estimate=cost(size * 24, size * 8),
    )(flip.reshape(1), *operands)


def spectrum_of(section, part, sides, flip):
    hosts, _, local, depth, width = section.shape
    count = hosts * local
    if depth % 8 or width % 128:
        flat = section[:, part].reshape(hosts // sides, sides, local, depth, width)
        flat = flat.transpose(1, 0, 2, 3, 4).reshape(count, 1, depth, width)
        return jnp.einsum("us,scpj->ucpj", flipped_matrix(count, flip), flat, precision=precise)

    def kernel(flip_ref, in_ref, out_ref):
        def body(lanes):
            def load(s):
                host, row = place_of(s, local, hosts, sides)
                return in_ref[host, 0, row, :, lanes]

            store_slots(out_ref, lanes, analyse(load, 0, 1, count), flip_ref[0])

        each_lane_tile(width, body)

    shape = (count, 1, depth, width)
    block = pl.BlockSpec((hosts, 1, local, 8, width), lambda t, _: (0, part, 0, t, 0))
    return tiles_call(kernel, flip, [section], [block], shape, slot_block(shape))


def sectors_of(spectrum, part, hosts, sides, flip):
    count, _, depth, width = spectrum.shape
    local = count // hosts
    shape = (hosts, local, depth, width)
    if depth % 8 or width % 128:
        flat = spectrum[:, part]
        flat = jnp.einsum("us,upj->spj", flipped_matrix(count, flip), flat, precision=precise)
        flat = flat.reshape(sides, hosts // sides, local, depth, width)
        return flat.transpose(1, 0, 2, 3, 4).reshape(shape)

    def kernel(flip_ref, in_ref, out_ref):
        def body(lanes):
            def emit(s, value):
                host, row = place_of(s, local, hosts, sides)
                out_ref[host, row, :, lanes] = value

            synthesise(load_slots(in_ref, lanes, count, flip_ref[0]), emit, 0, 1, count)

        each_lane_tile(width, body)

    block = pl.BlockSpec((hosts, local, 8, width), lambda t, _: (0, 0, t, 0))
    specs = [slot_block(spectrum.shape, part)]
    return tiles_call(kernel, flip, [spectrum], specs, shape, block)


def ratio_of(forward, measured, part, sides, flip):
    count, _, depth, width = forward.shape
    hosts, _, local = measured.shape[:3]
    scale = 1.0 / count
    shape = (count, 1, depth, width)
    if depth % 8 or width % 128:
        estimate = sectors_of(forward, part, hosts, sides, flip) * scale
        expected = jnp.maximum(estimate + measured[:, 1], 1.0)
        return spectrum_of((measured[:, 0] / expected * scale)[:, None], 0, sides, flip)

    def kernel(flip_ref, in_ref, measured_ref, out_ref, held):
        def body(lanes):
            def emit(s, value):
                host, row = place_of(s, local, hosts, sides)
                expected = jnp.maximum(value * scale + measured_ref[host, 1, row, :, lanes], 1.0)
                held[s] = measured_ref[host, 0, row, :, lanes] / expected * scale

            synthesise(load_slots(in_ref, lanes, count, flip_ref[0]), emit, 0, 1, count)
            spectrum = analyse(lambda s: held[s], 0, 1, count)
            store_slots(out_ref, lanes, spectrum, flip_ref[0])

        each_lane_tile(width, body)

    specs = [
        slot_block(forward.shape, part),
        pl.BlockSpec((hosts, 2, local, 8, width), lambda t, _: (0, 0, 0, t, 0)),
    ]
    scratch = [pltpu.VMEM((count, 8, 128), jnp.float32)]
    operands = [forward, measured]
    return tiles_call(kernel, flip, operands, specs, shape, slot_block(shape), scratch)


def masked_block(system, pattern, which):
    _, _, _, height, width = system.shape
    rows, cols = pattern.shape[2:]
    tile_height, tile_width = height // rows, width // cols

    def kernel(which_ref, pattern_ref, in_ref, out_ref):
        for row in range(rows):
            for col in range(cols):
                at = (slice(row * tile_height, (row + 1) * tile_height),)
                at += (slice(col * tile_width, (col + 1) * tile_width),)
                value = pattern_ref[(which_ref[0] * rows + row) * cols + col].astype(jnp.float32)
                out_ref[(0,) + at] = in_ref[(0, 0, 0) + at] * value

    return pl.pallas_call(
        kernel,
        grid_spec=pltpu.PrefetchScalarGridSpec(
            num_scalar_prefetch=2,
            grid=(2,),
            in_specs=[pl.BlockSpec((1, 1, 1, height, width), lambda a, w, _: (0, w[0], a, 0, 0))],
            out_specs=pl.BlockSpec((1, height, width), lambda a, w, _: (a, 0, 0)),
        ),
        out_shape=jax.ShapeDtypeStruct((2, height, width), jnp.float32),
        cost_estimate=cost(2 * height * width, 16 * height * width),
        compiler_params=tile_params(1),
        name="masked",
    )(which.reshape(1), pattern.reshape(-1), system)


def split(value):
    high = value.astype(jnp.bfloat16)
    return high, (value - high.astype(jnp.float32)).astype(jnp.bfloat16)


def folded(first, second, weights):
    own, other, sign = weights[0], weights[1], weights[2]
    upper = own * first[0] + other * second[0]
    lower = other * first[0] + own * second[0]
    return upper, lower, sign * (first[1] - second[1])


def operator_of(first, second, weights, adjoint):
    height, inner = first.shape[1:]
    if height % 128 or inner % 128:
        upper, lower, cross = folded(first, second, weights)
        if adjoint:
            table = jnp.block([[upper, -cross], [cross, lower]])
        else:
            table = jnp.block([[upper.T, cross.T], [-cross.T, lower.T]])
        return split(table)
    shape = (2 * height, 2 * inner) if adjoint else (2 * inner, 2 * height)

    def kernel(weights_ref, first_ref, second_ref, high_ref, low_ref):
        def put(at, value):
            high_ref[at], low_ref[at] = split(value)

        index = pl.program_id(0)
        at = pl.ds(pl.multiple_of(index * 128, 128), 128)
        at2 = pl.ds(pl.multiple_of(index * 128 + height, 128), 128)
        upper, lower, cross = folded(first_ref, second_ref, weights_ref)
        one, two = slice(0, inner), slice(inner, 2 * inner)
        if adjoint:
            put((at, one), upper)
            put((at, two), -cross)
            put((at2, one), cross)
            put((at2, two), lower)
        else:
            cross = cross.T
            put((one, at), upper.T)
            put((one, at2), cross)
            put((two, at), -cross)
            put((two, at2), lower.T)

    return pl.pallas_call(
        kernel,
        grid_spec=pltpu.PrefetchScalarGridSpec(
            num_scalar_prefetch=1,
            grid=(height // 128,),
            in_specs=[pl.BlockSpec((2, 128, inner), lambda t, w: (0, t, 0))] * 2,
            out_specs=[pl.BlockSpec(shape, lambda t, w: (0, 0))] * 2,
        ),
        out_shape=[jax.ShapeDtypeStruct(shape, jnp.bfloat16)] * 2,
        compiler_params=tile_params(1),
        cost_estimate=cost(16 * height * inner, 32 * height * inner),
        name="operator",
    )(weights, first, second)


def apply_operators(operators, spectra):
    hosts, reals, parts, depth, width = spectra.shape
    slots = reals // 2
    result = operators[0][0].shape[1] // 2
    if depth % 8 or width % 128 or result % 256:
        outs = []
        for slot, (high, low) in enumerate(operators):
            table = high.astype(jnp.float32) + low.astype(jnp.float32)
            rows = jnp.concatenate([spectra[:, 2 * slot], spectra[:, 2 * slot + 1]], axis=-1)
            out = jnp.einsum("ncpi,ij->ncpj", rows, table, precision=precise)
            outs += [out[..., :result], out[..., result:]]
        return jnp.stack(outs, axis=1)

    panel, per_part = 256, result // 256
    group = hosts
    while group * parts * depth > 256 and group % 2 == 0:
        group //= 2
    rows = group * parts * depth

    def kernel(*refs):
        terms, in_ref, out_ref, lhs_high, lhs_low = refs[: 2 * slots], *refs[2 * slots :]

        @pl.when(pl.program_id(0) == 0)
        def _():
            for slot in range(slots):
                for part in range(2):
                    lanes = slice(part * width, (part + 1) * width)
                    value = in_ref[:, 2 * slot + part].reshape(hosts * parts * depth, width)
                    lhs_high[slot, :, lanes], lhs_low[slot, :, lanes] = split(value)

        dot = functools.partial(jnp.dot, preferred_element_type=jnp.float32)

        def multiply(index, carry):
            at = pl.ds(pl.multiple_of(index * rows, rows), rows)
            out_at = pl.ds(index * group, group)
            for slot in range(slots):
                high, low = terms[2 * slot][...], terms[2 * slot + 1][...]
                total = dot(lhs_high[slot, at, :], low) + dot(lhs_low[slot, at, :], high)
                total = total + dot(lhs_high[slot, at, :], high)
                out_ref[out_at, slot, 0] = total.reshape(group, parts, depth, panel)
            return carry

        lax.fori_loop(0, hosts // group, multiply, 0)

    shape = (hosts, slots, 2, parts, depth, result)
    out = pl.pallas_call(
        kernel,
        grid=(2 * per_part,),
        in_specs=[pl.BlockSpec((2 * width, panel), lambda t: (0, t))] * (2 * slots)
        + [pl.BlockSpec(spectra.shape, lambda t: (0, 0, 0, 0, 0))],
        out_specs=pl.BlockSpec(
            (hosts, slots, 1, parts, depth, panel),
            lambda t: (0, 0, t // per_part, 0, 0, t % per_part),
        ),
        out_shape=jax.ShapeDtypeStruct(shape, jnp.float32),
        scratch_shapes=[pltpu.VMEM((slots, hosts * parts * depth, 2 * width), jnp.bfloat16)] * 2,
        compiler_params=tile_params(1),
        cost_estimate=cost(24 * slots * hosts * parts * depth * width * result, 3 * 2**23),
    )(*[term for pair in operators for term in pair], spectra)
    return out.reshape(hosts, reals, parts, depth, result)


def upper_side(side, sides):
    return 2 * side >= sides


def routes(count, hosts, sides):
    local, slots, half = count // hosts, count // 2 // hosts, count // 2
    rounds = []
    for slot in range(slots):
        for turn in range(2):
            sent, direct, inside, across = [None] * (hosts * sides), [], [], []
            for g in range(sides):
                for i in range(hosts):
                    r = slots * i + slot
                    near, far = r, (count - r if r else half)
                    upper = upper_side(g, sides)
                    if upper:
                        near, far = half + r, (half - r) % half
                    k = far if (i + turn + g + upper) % 2 else near
                    host = k // local
                    source, middle = host * sides + g, host * sides // hosts * hosts + i
                    assert sent[source] is None
                    sent[source] = k % local
                    direct.append((source, g * hosts + i))
                    inside.append((source, middle))
                    across.append((middle, g * hosts + i))
            two_hops = len({middle for _, middle in inside}) == hosts * sides
            rounds.append((sent, [inside, across] if two_hops else [direct]))
    return rounds


def on_device(hosts, sides, activity, system, pattern, counts, background, sensitivity):
    local, frames, planes, image = activity.shape
    sino = system.shape[3]
    count = local * hosts
    slots = count // 2 // hosts
    share = planes // sides
    depth = frames * share // hosts
    device = lax.axis_index(BOTH)
    seg = lax.axis_index("seg")
    side, place = device // hosts, device % hosts
    flip = upper_side(side, sides).astype(jnp.int32)
    groups = [[g * hosts + i for i in range(hosts)] for g in range(sides)]
    within = hosts // sides
    swap = [
        ((a * within + f) * sides + b, (b * within + f) * sides + a)
        for a in range(sides)
        for f in range(within)
        for b in range(sides)
    ]

    def exchange_side(array):
        return lax.all_to_all(
            array, BOTH, split_axis=0, concat_axis=0, tiled=True, axis_index_groups=groups
        )

    def permute(array, pairs):
        return lax.ppermute(array, BOTH, pairs)

    columns = activity.reshape(local, frames, sides, share, image).transpose(2, 0, 1, 3, 4)
    columns = columns.reshape(sides, local, hosts, depth, image).transpose(2, 0, 1, 3, 4)
    columns = exchange_side(permute(columns, swap))

    odd = (place + side) % 2
    zero = slots * place + jnp.arange(slots) == 0
    own = jnp.where(zero & (odd == 1), 0.0, 1.0)
    other = jnp.where(zero & (odd == 0), 0.0, 1.0)
    sign = jnp.where(zero, 0.0, 1.0 - 2.0 * odd)
    weights = jnp.stack([own, other, sign], axis=1)

    blocks = []
    for sent, hops in routes(count, hosts, sides):
        block = masked_block(system, pattern, jnp.asarray(sent, jnp.int32)[device])
        for pairs in hops[:-1]:
            block = permute(block, pairs)
            block, weights = lax.optimization_barrier((block, weights))
        blocks.append(permute(block, hops[-1]))
    measured = jnp.stack([counts[0].astype(jnp.float32), background[0]])
    measured = measured.reshape(2, local, frames, sides, share, sino)
    parts = []
    for part in range(sides):
        array = measured[:, :, :, part].reshape(2, local, hosts, depth, sino)
        array = array.transpose(2, 0, 1, 3, 4)
        parts.append(exchange_side(permute(array, swap)))

    def by_owner(array):
        return array.reshape((hosts, 2 * slots) + array.shape[1:])

    def by_slot(array):
        return array.reshape((count,) + array.shape[2:])

    pairs = [(blocks[2 * slot], blocks[2 * slot + 1], weights[slot]) for slot in range(slots)]
    spectra = [spectrum_of(columns, part, sides, flip) for part in range(sides)]
    spectra = exchange_side(by_owner(jnp.concatenate(spectra, axis=1)))
    project = [operator_of(*pair, False) for pair in pairs]
    forward = by_slot(exchange_side(apply_operators(project, spectra)))
    adjoint = [operator_of(*pair, True) for pair in pairs]
    results = []
    for part in range(sides):
        ratio = ratio_of(forward, parts[part], part, sides, flip)
        spectra = exchange_side(by_owner(ratio))
        backward = apply_operators(adjoint, spectra)
        backward = by_slot(exchange_side(backward))
        back = sectors_of(backward, 0, hosts, sides, flip)
        results.append(permute(exchange_side(back), swap))
    back = lax.all_to_all(jnp.stack(results), "seg", split_axis=0, concat_axis=0, tiled=True)
    total = back.sum(0).transpose(1, 0, 2, 3).reshape(local, frames, share, image)
    current = lax.dynamic_slice_in_dim(activity, seg * share, share, 2)
    return current * total / sensitivity[:, None]


def solution(mesh):
    in_specs = (
        P("freq", None, None, None),
        P("seg", "freq", None, None, None),
        P("seg", "freq", None, None),
        P("seg", "freq", None, None, None),
        P("seg", "freq", None, None, None),
        P("freq", "seg", None),
    )
    hosts, sides = mesh.shape["freq"], mesh.shape["seg"]

    def body(activity, *rest):
        return on_device(hosts, sides, activity, *rest)

    return jax.shard_map(
        body, mesh=mesh, in_specs=in_specs, out_specs=P("freq", None, "seg", None), check_vma=False
    )
```

```python
import functools

import jax
import jax.numpy as jnp
import numpy as np
from jax import lax
from jax.experimental import pallas as pl
from jax.experimental.pallas import tpu as pltpu
from jax.sharding import PartitionSpec as P

BOTH = ("freq", "seg")
precise = lax.Precision.HIGHEST


def analyse(load, start, step, size):
    if size == 1:
        return [(load(start), None)]
    if size == 2:
        first, second = load(start), load(start + step)
        return [(first + second, None), (first - second, None)]
    even = analyse(load, start, 2 * step, size // 2)
    odd = analyse(load, start + step, 2 * step, size // 2)
    half, quarter = size // 2, size // 4
    out = [None] * (half + 1)
    out[0] = (even[0][0] + odd[0][0], None)
    out[half] = (even[0][0] - odd[0][0], None)
    out[quarter] = (even[quarter][0], -odd[quarter][0])
    for k in range(1, quarter):
        cosine, sine = float(np.cos(2 * np.pi * k / size)), float(np.sin(2 * np.pi * k / size))
        real, imag = odd[k]
        turned_real = real * cosine + imag * sine
        turned_imag = imag * cosine - real * sine
        out[k] = (even[k][0] + turned_real, even[k][1] + turned_imag)
        out[half - k] = (even[k][0] - turned_real, turned_imag - even[k][1])
    return out


def synthesise(values, emit, start, step, size):
    if size == 1:
        emit(start, values[0][0])
        return
    if size == 2:
        emit(start, values[0][0] + values[1][0])
        emit(start + step, values[0][0] - values[1][0])
        return
    half, quarter = size // 2, size // 4
    even, odd = [None] * (quarter + 1), [None] * (quarter + 1)
    even[0] = (values[0][0] + values[half][0], None)
    odd[0] = (values[0][0] - values[half][0], None)
    even[quarter] = (values[quarter][0], None)
    odd[quarter] = (-values[quarter][1], None)
    for k in range(1, quarter):
        cosine, sine = float(np.cos(2 * np.pi * k / size)), float(np.sin(2 * np.pi * k / size))
        (real, imag), (other_real, other_imag) = values[k], values[half - k]
        even[k] = (real + other_real, imag - other_imag)
        diff_real, diff_imag = real - other_real, imag + other_imag
        odd[k] = (diff_real * cosine - diff_imag * sine, diff_real * sine + diff_imag * cosine)
    synthesise(even, emit, start, 2 * step, half)
    synthesise(odd, emit, start + step, 2 * step, half)


def analysis_matrix(size):
    angles = 2 * np.pi * np.outer(np.arange(size // 2), np.arange(size)) / size
    table = np.stack([np.cos(angles), -np.sin(angles)], axis=1).reshape(size, size)
    table[1] = np.where(np.arange(size) % 2 == 0, 1.0, -1.0)
    return jnp.asarray(table, jnp.float32)


def slot_index(k, half, flip):
    return k + flip * ((half - k) % half - k)


def load_slots(ref, lanes, size, flip):
    half = size // 2
    at = [2 * slot_index(k, half, flip) for k in range(half)]
    values = [(ref[row, 0, :, lanes], ref[row + 1, 0, :, lanes]) for row in at]
    return [(values[0][0], None)] + values[1:] + [(values[0][1], None)]


def store_slots(ref, lanes, spectrum, flip):
    half = len(spectrum) - 1
    ref[0, 0, :, lanes] = spectrum[0][0]
    ref[1, 0, :, lanes] = spectrum[half][0]
    for k in range(1, half):
        row = 2 * slot_index(k, half, flip)
        ref[row, 0, :, lanes] = spectrum[k][0]
        ref[row + 1, 0, :, lanes] = spectrum[k][1]


def flipped_matrix(size, flip):
    table = analysis_matrix(size).reshape(size // 2, 2, size)
    order = slot_index(np.arange(size // 2), size // 2, flip)
    return table[order].reshape(size, size)


def each_lane_tile(width, body):
    def step(index, carry):
        body(pl.ds(pl.multiple_of(index * 128, 128), 128))
        return carry

    lax.fori_loop(0, width // 128, step, 0)


def tile_params(axes):
    return pltpu.CompilerParams(dimension_semantics=("arbitrary",) * axes)


def cost(flops, nbytes):
    return pl.CostEstimate(flops=int(flops), bytes_accessed=int(nbytes), transcendentals=0)


def slot_block(shape, part=0):
    count, _, _, width = shape
    return pl.BlockSpec((count, 1, 8, width), lambda t, _: (0, part, t, 0))


def place_of(s, local, hosts, sides):
    host, within = s // local, hosts // sides
    return host % within * sides + host // within, s % local


def tiles_call(kernel, flip, operands, in_specs, shape, out_spec, scratch=()):
    steps = operands[0].shape[-2] // 8
    size = sum(operand.size for operand in operands)
    return pl.pallas_call(
        kernel,
        grid_spec=pltpu.PrefetchScalarGridSpec(
            num_scalar_prefetch=1,
            grid=(steps,),
            in_specs=in_specs,
            out_specs=out_spec,
            scratch_shapes=scratch,
        ),
        out_shape=jax.ShapeDtypeStruct(shape, jnp.float32),
        compiler_params=tile_params(1),
        cost_estimate=cost(size * 24, size * 8),
    )(flip.reshape(1), *operands)


def spectrum_of(section, part, sides, flip):
    hosts, _, local, depth, width = section.shape
    count = hosts * local
    if depth % 8 or width % 128:
        flat = section[:, part].reshape(hosts // sides, sides, local, depth, width)
        flat = flat.transpose(1, 0, 2, 3, 4).reshape(count, 1, depth, width)
        return jnp.einsum("us,scpj->ucpj", flipped_matrix(count, flip), flat, precision=precise)

    def kernel(flip_ref, in_ref, out_ref):
        def body(lanes):
            def load(s):
                host, row = place_of(s, local, hosts, sides)
                return in_ref[host, 0, row, :, lanes]

            store_slots(out_ref, lanes, analyse(load, 0, 1, count), flip_ref[0])

        each_lane_tile(width, body)

    shape = (count, 1, depth, width)
    block = pl.BlockSpec((hosts, 1, local, 8, width), lambda t, _: (0, part, 0, t, 0))
    return tiles_call(kernel, flip, [section], [block], shape, slot_block(shape))


def sectors_of(spectrum, part, hosts, sides, flip):
    count, _, depth, width = spectrum.shape
    local = count // hosts
    shape = (hosts, local, depth, width)
    if depth % 8 or width % 128:
        flat = spectrum[:, part]
        flat = jnp.einsum("us,upj->spj", flipped_matrix(count, flip), flat, precision=precise)
        flat = flat.reshape(sides, hosts // sides, local, depth, width)
        return flat.transpose(1, 0, 2, 3, 4).reshape(shape)

    def kernel(flip_ref, in_ref, out_ref):
        def body(lanes):
            def emit(s, value):
                host, row = place_of(s, local, hosts, sides)
                out_ref[host, row, :, lanes] = value

            synthesise(load_slots(in_ref, lanes, count, flip_ref[0]), emit, 0, 1, count)

        each_lane_tile(width, body)

    block = pl.BlockSpec((hosts, local, 8, width), lambda t, _: (0, 0, t, 0))
    specs = [slot_block(spectrum.shape, part)]
    return tiles_call(kernel, flip, [spectrum], specs, shape, block)


def ratio_of(forward, measured, part, sides, flip):
    count, _, depth, width = forward.shape
    hosts, _, local = measured.shape[:3]
    scale = 1.0 / count
    shape = (count, 1, depth, width)
    if depth % 8 or width % 128:
        estimate = sectors_of(forward, part, hosts, sides, flip) * scale
        expected = jnp.maximum(estimate + measured[:, 1], 1.0)
        return spectrum_of((measured[:, 0] / expected * scale)[:, None], 0, sides, flip)

    def kernel(flip_ref, in_ref, measured_ref, out_ref, held):
        def body(lanes):
            def emit(s, value):
                host, row = place_of(s, local, hosts, sides)
                expected = jnp.maximum(value * scale + measured_ref[host, 1, row, :, lanes], 1.0)
                held[s] = measured_ref[host, 0, row, :, lanes] / expected * scale

            synthesise(load_slots(in_ref, lanes, count, flip_ref[0]), emit, 0, 1, count)
            spectrum = analyse(lambda s: held[s], 0, 1, count)
            store_slots(out_ref, lanes, spectrum, flip_ref[0])

        each_lane_tile(width, body)

    specs = [
        slot_block(forward.shape, part),
        pl.BlockSpec((hosts, 2, local, 8, width), lambda t, _: (0, 0, 0, t, 0)),
    ]
    scratch = [pltpu.VMEM((count, 8, 128), jnp.float32)]
    operands = [forward, measured]
    return tiles_call(kernel, flip, operands, specs, shape, slot_block(shape), scratch)


def masked_block(system, pattern, which):
    _, _, _, height, width = system.shape
    rows, cols = pattern.shape[2:]
    tile_height, tile_width = height // rows, width // cols

    def kernel(which_ref, pattern_ref, in_ref, out_ref):
        for row in range(rows):
            for col in range(cols):
                at = (slice(row * tile_height, (row + 1) * tile_height),)
                at += (slice(col * tile_width, (col + 1) * tile_width),)
                value = pattern_ref[(which_ref[0] * rows + row) * cols + col].astype(jnp.float32)
                out_ref[(0,) + at] = in_ref[(0, 0, 0) + at] * value

    return pl.pallas_call(
        kernel,
        grid_spec=pltpu.PrefetchScalarGridSpec(
            num_scalar_prefetch=2,
            grid=(2,),
            in_specs=[pl.BlockSpec((1, 1, 1, height, width), lambda a, w, _: (0, w[0], a, 0, 0))],
            out_specs=pl.BlockSpec((1, height, width), lambda a, w, _: (a, 0, 0)),
        ),
        out_shape=jax.ShapeDtypeStruct((2, height, width), jnp.float32),
        cost_estimate=cost(2 * height * width, 16 * height * width),
        compiler_params=tile_params(1),
        name="masked",
    )(which.reshape(1), pattern.reshape(-1), system)


def split(value):
    high = value.astype(jnp.bfloat16)
    return high, (value - high.astype(jnp.float32)).astype(jnp.bfloat16)


def folded(first, second, weights):
    own, other, sign = weights[0], weights[1], weights[2]
    upper = own * first[0] + other * second[0]
    lower = other * first[0] + own * second[0]
    return upper, lower, sign * (first[1] - second[1])


def operator_of(first, second, weights, adjoint):
    height, inner = first.shape[1:]
    if height % 128 or inner % 128:
        upper, lower, cross = folded(first, second, weights)
        if adjoint:
            table = jnp.block([[upper, -cross], [cross, lower]])
        else:
            table = jnp.block([[upper.T, cross.T], [-cross.T, lower.T]])
        return split(table)
    shape = (2 * height, 2 * inner) if adjoint else (2 * inner, 2 * height)

    def kernel(weights_ref, first_ref, second_ref, high_ref, low_ref):
        def put(at, value):
            high_ref[at], low_ref[at] = split(value)

        index = pl.program_id(0)
        at = pl.ds(pl.multiple_of(index * 128, 128), 128)
        at2 = pl.ds(pl.multiple_of(index * 128 + height, 128), 128)
        upper, lower, cross = folded(first_ref, second_ref, weights_ref)
        one, two = slice(0, inner), slice(inner, 2 * inner)
        if adjoint:
            put((at, one), upper)
            put((at, two), -cross)
            put((at2, one), cross)
            put((at2, two), lower)
        else:
            cross = cross.T
            put((one, at), upper.T)
            put((one, at2), cross)
            put((two, at), -cross)
            put((two, at2), lower.T)

    return pl.pallas_call(
        kernel,
        grid_spec=pltpu.PrefetchScalarGridSpec(
            num_scalar_prefetch=1,
            grid=(height // 128,),
            in_specs=[pl.BlockSpec((2, 128, inner), lambda t, w: (0, t, 0))] * 2,
            out_specs=[pl.BlockSpec(shape, lambda t, w: (0, 0))] * 2,
        ),
        out_shape=[jax.ShapeDtypeStruct(shape, jnp.bfloat16)] * 2,
        compiler_params=tile_params(1),
        cost_estimate=cost(16 * height * inner, 32 * height * inner),
        name="operator",
    )(weights, first, second)


def apply_operators(operators, spectra):
    hosts, reals, parts, depth, width = spectra.shape
    slots = reals // 2
    result = operators[0][0].shape[1] // 2
    if depth % 8 or width % 128 or result % 256:
        outs = []
        for slot, (high, low) in enumerate(operators):
            table = high.astype(jnp.float32) + low.astype(jnp.float32)
            rows = jnp.concatenate([spectra[:, 2 * slot], spectra[:, 2 * slot + 1]], axis=-1)
            out = jnp.einsum("ncpi,ij->ncpj", rows, table, precision=precise)
            outs += [out[..., :result], out[..., result:]]
        return jnp.stack(outs, axis=1)

    panel, per_part = 256, result // 256
    group = hosts
    while group * parts * depth > 256 and group % 2 == 0:
        group //= 2
    rows = group * parts * depth

    def kernel(*refs):
        terms, in_ref, out_ref, lhs_high, lhs_low = refs[: 2 * slots], *refs[2 * slots :]

        @pl.when(pl.program_id(0) == 0)
        def _():
            for slot in range(slots):
                for part in range(2):
                    lanes = slice(part * width, (part + 1) * width)
                    value = in_ref[:, 2 * slot + part].reshape(hosts * parts * depth, width)
                    lhs_high[slot, :, lanes], lhs_low[slot, :, lanes] = split(value)

        dot = functools.partial(jnp.dot, preferred_element_type=jnp.float32)

        def multiply(index, carry):
            at = pl.ds(pl.multiple_of(index * rows, rows), rows)
            out_at = pl.ds(index * group, group)
            for slot in range(slots):
                high, low = terms[2 * slot][...], terms[2 * slot + 1][...]
                total = dot(lhs_high[slot, at, :], low) + dot(lhs_low[slot, at, :], high)
                total = total + dot(lhs_high[slot, at, :], high)
                out_ref[out_at, slot, 0] = total.reshape(group, parts, depth, panel)
            return carry

        lax.fori_loop(0, hosts // group, multiply, 0)

    shape = (hosts, slots, 2, parts, depth, result)
    out = pl.pallas_call(
        kernel,
        grid=(2 * per_part,),
        in_specs=[pl.BlockSpec((2 * width, panel), lambda t: (0, t))] * (2 * slots)
        + [pl.BlockSpec(spectra.shape, lambda t: (0, 0, 0, 0, 0))],
        out_specs=pl.BlockSpec(
            (hosts, slots, 1, parts, depth, panel),
            lambda t: (0, 0, t // per_part, 0, 0, t % per_part),
        ),
        out_shape=jax.ShapeDtypeStruct(shape, jnp.float32),
        scratch_shapes=[pltpu.VMEM((slots, hosts * parts * depth, 2 * width), jnp.bfloat16)] * 2,
        compiler_params=tile_params(1),
        cost_estimate=cost(24 * slots * hosts * parts * depth * width * result, 3 * 2**23),
    )(*[term for pair in operators for term in pair], spectra)
    return out.reshape(hosts, reals, parts, depth, result)


def upper_side(side, sides):
    return 2 * side >= sides


def routes(count, hosts, sides):
    local, slots, half = count // hosts, count // 2 // hosts, count // 2
    within = hosts // sides
    rounds = []
    for slot in range(slots):
        for turn in range(2):
            sent, direct, inside = [None] * (hosts * sides), [], []
            for g in range(sides):
                for i in range(hosts):
                    r = slots * i + slot
                    near, far = r, (count - r if r else half)
                    upper = upper_side(g, sides)
                    if upper:
                        near, far = half + r, (half - r) % half
                    is_far = (i + turn + g + upper) % 2
                    k = far if is_far else near
                    host = k // local
                    source, origin, place = host * sides + g, host // within, i
                    if is_far:
                        place = (i + hosts // 2) % hosts
                    assert sent[source] is None
                    sent[source] = k % local
                    direct.append((source, g * hosts + i))
                    inside.append((source, origin * hosts + place))
            rounds.append((sent, direct, inside))
    return rounds


def on_device(hosts, sides, activity, system, pattern, counts, background, sensitivity):
    local, frames, planes, image = activity.shape
    sino = system.shape[3]
    count = local * hosts
    slots = count // 2 // hosts
    share = planes // sides
    depth = frames * share // hosts
    within = hosts // sides
    device = lax.axis_index(BOTH)
    seg = lax.axis_index("seg")
    side, place = device // hosts, device % hosts
    flip = upper_side(side, sides).astype(jnp.int32)
    groups = [[g * hosts + i for i in range(hosts)] for g in range(sides)]
    swap = [
        ((a * within + f) * sides + b, (b * within + f) * sides + a)
        for a in range(sides)
        for f in range(within)
        for b in range(sides)
        if a != b
    ]

    def permute(array, pairs):
        return lax.ppermute(array, BOTH, pairs)

    def swapped(array, moved):
        return jnp.where(side == seg, array, moved)

    def exchange(array):
        return lax.all_to_all(
            array, BOTH, split_axis=0, concat_axis=0, tiled=True, axis_index_groups=groups
        )

    current = lax.dynamic_slice_in_dim(activity, seg * share, share, 2)
    columns = current.reshape(local, hosts, depth, image).transpose(1, 0, 2, 3)
    columns = jnp.broadcast_to(columns[None], (sides,) + columns.shape)
    columns = columns.reshape(sides * hosts, local, depth, image)
    columns = lax.all_to_all(columns, BOTH, split_axis=0, concat_axis=0, tiled=True)
    columns = columns.reshape(hosts, sides, local, depth, image)

    measured = jnp.stack([counts[0].astype(jnp.float32), background[0]])
    measured = measured.reshape(2, local, frames, sides, share, sino)
    parts = [measured[:, :, :, part].reshape(2, local, hosts, depth, sino) for part in range(sides)]
    parts = [part.transpose(2, 0, 1, 3, 4) for part in parts]

    tables = routes(count, hosts, sides)
    masked = [
        masked_block(system, pattern, jnp.asarray(sent, jnp.int32)[device])
        for sent, _, _ in tables
    ]
    zero = slots * place + jnp.arange(slots) == 0
    if sides == 2:
        moved = []
        for turn, (_, _, inside) in enumerate(tables):
            pairs = [pair for pair in inside if pair[0] != pair[1]]
            stays = [0] * (hosts * sides)
            for source, target in inside:
                stays[target] = int(source == target)
            got = permute(masked[turn], pairs)
            moved.append(jnp.where(jnp.asarray(stays)[device] == 1, masked[turn], got))
        near, far = [], []
        for slot in range(slots):
            got = moved[2 * slot : 2 * slot + 2]
            near.append(jnp.where(seg == 0, got[0], got[1]))
            far.append(jnp.where(seg == 0, got[1], got[0]))
        across = []
        for i in range(hosts):
            other = (i + hosts // 2) % hosts
            across += [(other, hosts + i), (hosts + other, i)]
        columns, parts[0], near, far = lax.optimization_barrier((columns, parts[0], near, far))
        arrived = permute(parts[0], swap)
        arrived, far[0] = lax.optimization_barrier((arrived, far[0]))
        parts[0] = exchange(swapped(parts[0], arrived))
        for slot in range(slots):
            far[slot] = permute(far[slot], across)
            if slot + 1 < slots:
                far[slot], far[slot + 1] = lax.optimization_barrier((far[slot], far[slot + 1]))
        far[-1], parts[1] = lax.optimization_barrier((far[-1], parts[1]))
        arrived = permute(parts[1], swap)
        parts[1] = exchange(swapped(parts[1], arrived))
        blocks = list(zip(near, far))
        odd = flip
    else:
        moved = [lax.ppermute(block, BOTH, table[1]) for block, table in zip(masked, tables)]
        blocks = [moved[2 * slot : 2 * slot + 2] for slot in range(slots)]
        for part in range(sides):
            arrived = permute(parts[part], swap)
            parts[part] = exchange(swapped(parts[part], arrived))
        odd = (place + side) % 2
    own = jnp.where(zero & (odd == 1), 0.0, 1.0)
    other = jnp.where(zero & (odd == 0), 0.0, 1.0)
    sign = jnp.where(zero, 0.0, 1.0 - 2.0 * odd)
    weights = jnp.stack([own, other, sign], axis=1)
    blocks = [(*pair, weights[slot]) for slot, pair in enumerate(blocks)]

    def by_owner(array):
        return array.reshape((hosts, 2 * slots) + array.shape[1:])

    def by_slot(array):
        return array.reshape((count,) + array.shape[2:])

    spectra = [spectrum_of(columns, part, 1, flip) for part in range(sides)]
    spectra = by_owner(jnp.concatenate(spectra, axis=1))
    spectra = exchange(spectra)
    forward = []
    for slot in range(slots):
        operator = [operator_of(*blocks[slot], False)]
        pair = apply_operators(operator, spectra[:, 2 * slot : 2 * slot + 2])
        forward.append(exchange(pair))
    forward = by_slot(jnp.concatenate(forward, axis=1))
    adjoint = [operator_of(*block, True) for block in blocks]
    results = []
    for part in range(sides):
        ratio = ratio_of(forward, parts[part], part, sides, flip)
        spectra = exchange(by_owner(ratio))
        backward = apply_operators(adjoint, spectra)
        backward = by_slot(exchange(backward))
        back = sectors_of(backward, 0, hosts, sides, flip)
        back = exchange(back)
        results.append(swapped(back, permute(back, swap)))
    back = lax.all_to_all(jnp.stack(results), "seg", split_axis=0, concat_axis=0, tiled=True)
    total = back.sum(0).transpose(1, 0, 2, 3).reshape(local, frames, share, image)
    return current * total / sensitivity[:, None]


def solution(mesh):
    in_specs = (
        P("freq", None, None, None),
        P("seg", "freq", None, None, None),
        P("seg", "freq", None, None),
        P("seg", "freq", None, None, None),
        P("seg", "freq", None, None, None),
        P("freq", "seg", None),
    )
    hosts, sides = mesh.shape["freq"], mesh.shape["seg"]

    def body(activity, *rest):
        return on_device(hosts, sides, activity, *rest)

    return jax.shard_map(
        body, mesh=mesh, in_specs=in_specs, out_specs=P("freq", None, "seg", None), check_vma=False
    )
```

```python
import functools

import jax
import jax.numpy as jnp
import numpy as np
from jax import lax
from jax.experimental import pallas as pl
from jax.experimental.pallas import tpu as pltpu
from jax.sharding import PartitionSpec as P

BOTH = ("freq", "seg")
precise = lax.Precision.HIGHEST


def analyse(load, start, step, size):
    if size == 1:
        return [(load(start), None)]
    if size == 2:
        first, second = load(start), load(start + step)
        return [(first + second, None), (first - second, None)]
    even = analyse(load, start, 2 * step, size // 2)
    odd = analyse(load, start + step, 2 * step, size // 2)
    half, quarter = size // 2, size // 4
    out = [None] * (half + 1)
    out[0] = (even[0][0] + odd[0][0], None)
    out[half] = (even[0][0] - odd[0][0], None)
    out[quarter] = (even[quarter][0], -odd[quarter][0])
    for k in range(1, quarter):
        cosine, sine = float(np.cos(2 * np.pi * k / size)), float(np.sin(2 * np.pi * k / size))
        real, imag = odd[k]
        turned_real = real * cosine + imag * sine
        turned_imag = imag * cosine - real * sine
        out[k] = (even[k][0] + turned_real, even[k][1] + turned_imag)
        out[half - k] = (even[k][0] - turned_real, turned_imag - even[k][1])
    return out


def synthesise(values, emit, start, step, size):
    if size == 1:
        emit(start, values[0][0])
        return
    if size == 2:
        emit(start, values[0][0] + values[1][0])
        emit(start + step, values[0][0] - values[1][0])
        return
    half, quarter = size // 2, size // 4
    even, odd = [None] * (quarter + 1), [None] * (quarter + 1)
    even[0] = (values[0][0] + values[half][0], None)
    odd[0] = (values[0][0] - values[half][0], None)
    even[quarter] = (values[quarter][0], None)
    odd[quarter] = (-values[quarter][1], None)
    for k in range(1, quarter):
        cosine, sine = float(np.cos(2 * np.pi * k / size)), float(np.sin(2 * np.pi * k / size))
        (real, imag), (other_real, other_imag) = values[k], values[half - k]
        even[k] = (real + other_real, imag - other_imag)
        diff_real, diff_imag = real - other_real, imag + other_imag
        odd[k] = (diff_real * cosine - diff_imag * sine, diff_real * sine + diff_imag * cosine)
    synthesise(even, emit, start, 2 * step, half)
    synthesise(odd, emit, start + step, 2 * step, half)


def analysis_matrix(size):
    angles = 2 * np.pi * np.outer(np.arange(size // 2), np.arange(size)) / size
    table = np.stack([np.cos(angles), -np.sin(angles)], axis=1).reshape(size, size)
    table[1] = np.where(np.arange(size) % 2 == 0, 1.0, -1.0)
    return jnp.asarray(table, jnp.float32)


def slot_index(k, half, flip):
    return k + flip * ((half - k) % half - k)


def load_slots(ref, lanes, size, flip):
    half = size // 2
    at = [2 * slot_index(k, half, flip) for k in range(half)]
    values = [(ref[row, 0, :, lanes], ref[row + 1, 0, :, lanes]) for row in at]
    return [(values[0][0], None)] + values[1:] + [(values[0][1], None)]


def store_slots(ref, lanes, spectrum, flip):
    half = len(spectrum) - 1
    ref[0, 0, :, lanes] = spectrum[0][0]
    ref[1, 0, :, lanes] = spectrum[half][0]
    for k in range(1, half):
        row = 2 * slot_index(k, half, flip)
        ref[row, 0, :, lanes] = spectrum[k][0]
        ref[row + 1, 0, :, lanes] = spectrum[k][1]


def flipped_matrix(size, flip):
    table = analysis_matrix(size).reshape(size // 2, 2, size)
    order = slot_index(np.arange(size // 2), size // 2, flip)
    return table[order].reshape(size, size)


def each_lane_tile(width, body):
    def step(index, carry):
        body(pl.ds(pl.multiple_of(index * 128, 128), 128))
        return carry

    lax.fori_loop(0, width // 128, step, 0)


def tile_params(axes):
    return pltpu.CompilerParams(dimension_semantics=("arbitrary",) * axes)


def cost(flops, nbytes):
    return pl.CostEstimate(flops=int(flops), bytes_accessed=int(nbytes), transcendentals=0)


def slot_block(shape):
    count, _, _, width = shape
    return pl.BlockSpec((count, 1, 8, width), lambda c, t, _: (0, c, t, 0))


def sector_block(shape):
    hosts, _, local, _, width = shape
    return pl.BlockSpec((hosts, 1, local, 8, width), lambda c, t, _: (0, c, 0, t, 0))


def tiles_call(kernel, flip, operands, in_specs, shape, out_spec, scratch=()):
    parts, depth = operands[0].shape[1], operands[0].shape[-2]
    size = sum(operand.size for operand in operands)
    return pl.pallas_call(
        kernel,
        grid_spec=pltpu.PrefetchScalarGridSpec(
            num_scalar_prefetch=1,
            grid=(parts, depth // 8),
            in_specs=in_specs,
            out_specs=out_spec,
            scratch_shapes=scratch,
        ),
        out_shape=jax.ShapeDtypeStruct(shape, jnp.float32),
        compiler_params=tile_params(2),
        cost_estimate=cost(size * 24, size * 8),
    )(flip.reshape(1), *operands)


def spectrum_of(section, flip):
    hosts, parts, local, depth, width = section.shape
    count = hosts * local
    shape = (count, parts, depth, width)
    if depth % 8 or width % 128:
        flat = section.transpose(0, 2, 1, 3, 4).reshape(shape)
        return jnp.einsum("us,scpj->ucpj", flipped_matrix(count, flip), flat, precision=precise)

    def kernel(flip_ref, in_ref, out_ref):
        def body(lanes):
            load = lambda s: in_ref[s // local, 0, s % local, :, lanes]
            store_slots(out_ref, lanes, analyse(load, 0, 1, count), flip_ref[0])

        each_lane_tile(width, body)

    specs = [sector_block(section.shape)]
    return tiles_call(kernel, flip, [section], specs, shape, slot_block(shape))


def sectors_of(spectrum, hosts, flip):
    count, parts, depth, width = spectrum.shape
    local = count // hosts
    shape = (hosts, parts, local, depth, width)
    if depth % 8 or width % 128:
        table = flipped_matrix(count, flip)
        flat = jnp.einsum("us,ucpj->scpj", table, spectrum, precision=precise)
        return flat.reshape(hosts, local, parts, depth, width).transpose(0, 2, 1, 3, 4)

    def kernel(flip_ref, in_ref, out_ref):
        def body(lanes):
            def emit(s, value):
                out_ref[s // local, 0, s % local, :, lanes] = value

            synthesise(load_slots(in_ref, lanes, count, flip_ref[0]), emit, 0, 1, count)

        each_lane_tile(width, body)

    specs = [slot_block(spectrum.shape)]
    return tiles_call(kernel, flip, [spectrum], specs, shape, sector_block(shape))


def ratio_of(forward, measured, flip):
    count, _, depth, width = forward.shape
    hosts, _, _, local = measured.shape[:4]
    scale = 1.0 / count
    if depth % 8 or width % 128:
        estimate = sectors_of(forward, hosts, flip) * scale
        expected = jnp.maximum(estimate + measured[:, :, 1], 1.0)
        return spectrum_of(measured[:, :, 0] / expected * scale, flip)

    def kernel(flip_ref, in_ref, measured_ref, out_ref, held):
        def body(lanes):
            def emit(s, value):
                host, row = s // local, s % local
                expected = jnp.maximum(value * scale + measured_ref[host, 0, 1, row, :, lanes], 1.0)
                held[s] = measured_ref[host, 0, 0, row, :, lanes] / expected * scale

            synthesise(load_slots(in_ref, lanes, count, flip_ref[0]), emit, 0, 1, count)
            spectrum = analyse(lambda s: held[s], 0, 1, count)
            store_slots(out_ref, lanes, spectrum, flip_ref[0])

        each_lane_tile(width, body)

    block = pl.BlockSpec((hosts, 1, 2, local, 8, width), lambda c, t, _: (0, c, 0, 0, t, 0))
    specs = [slot_block(forward.shape), block]
    scratch = [pltpu.VMEM((count, 8, 128), jnp.float32)]
    operands, out = [forward, measured], slot_block(forward.shape)
    return tiles_call(kernel, flip, operands, specs, forward.shape, out, scratch)


def masked_block(system, pattern, which):
    _, _, _, height, width = system.shape
    rows, cols = pattern.shape[2:]
    tile_height, tile_width = height // rows, width // cols

    def kernel(which_ref, pattern_ref, in_ref, out_ref):
        for row in range(rows):
            for col in range(cols):
                at = (slice(row * tile_height, (row + 1) * tile_height),)
                at += (slice(col * tile_width, (col + 1) * tile_width),)
                value = pattern_ref[(which_ref[0] * rows + row) * cols + col].astype(jnp.float32)
                out_ref[(0,) + at] = in_ref[(0, 0, 0) + at] * value

    return pl.pallas_call(
        kernel,
        grid_spec=pltpu.PrefetchScalarGridSpec(
            num_scalar_prefetch=2,
            grid=(2,),
            in_specs=[pl.BlockSpec((1, 1, 1, height, width), lambda a, w, _: (0, w[0], a, 0, 0))],
            out_specs=pl.BlockSpec((1, height, width), lambda a, w, _: (a, 0, 0)),
        ),
        out_shape=jax.ShapeDtypeStruct((2, height, width), jnp.float32),
        cost_estimate=cost(2 * height * width, 16 * height * width),
        compiler_params=tile_params(1),
        name="masked",
    )(which.reshape(1), pattern.reshape(-1), system)


def split(value):
    high = value.astype(jnp.bfloat16)
    return high, (value - high.astype(jnp.float32)).astype(jnp.bfloat16)


def folded(first, second, weights):
    own, other, sign = weights[0], weights[1], weights[2]
    upper = own * first[0] + other * second[0]
    lower = other * first[0] + own * second[0]
    return upper, lower, sign * (first[1] - second[1])


def operator_of(first, second, weights, adjoint):
    height, inner = first.shape[1:]
    if height % 128 or inner % 128:
        upper, lower, cross = folded(first, second, weights)
        if adjoint:
            table = jnp.block([[upper, -cross], [cross, lower]])
        else:
            table = jnp.block([[upper.T, cross.T], [-cross.T, lower.T]])
        return split(table)
    shape = (2 * height, 2 * inner) if adjoint else (2 * inner, 2 * height)

    def kernel(weights_ref, first_ref, second_ref, high_ref, low_ref):
        def put(at, value):
            high_ref[at], low_ref[at] = split(value)

        index = pl.program_id(0)
        at = pl.ds(pl.multiple_of(index * 128, 128), 128)
        at2 = pl.ds(pl.multiple_of(index * 128 + height, 128), 128)
        upper, lower, cross = folded(first_ref, second_ref, weights_ref)
        one, two = slice(0, inner), slice(inner, 2 * inner)
        if adjoint:
            put((at, one), upper)
            put((at, two), -cross)
            put((at2, one), cross)
            put((at2, two), lower)
        else:
            cross = cross.T
            put((one, at), upper.T)
            put((one, at2), cross)
            put((two, at), -cross)
            put((two, at2), lower.T)

    return pl.pallas_call(
        kernel,
        grid_spec=pltpu.PrefetchScalarGridSpec(
            num_scalar_prefetch=1,
            grid=(height // 128,),
            in_specs=[pl.BlockSpec((2, 128, inner), lambda t, w: (0, t, 0))] * 2,
            out_specs=[pl.BlockSpec(shape, lambda t, w: (0, 0))] * 2,
        ),
        out_shape=[jax.ShapeDtypeStruct(shape, jnp.bfloat16)] * 2,
        compiler_params=tile_params(1),
        cost_estimate=cost(16 * height * inner, 32 * height * inner),
        name="operator",
    )(weights, first, second)


def apply_operators(operators, spectra):
    hosts, reals, parts, depth, width = spectra.shape
    slots = reals // 2
    result = operators[0][0].shape[1] // 2
    if depth % 8 or width % 128 or result % 256:
        outs = []
        for slot, (high, low) in enumerate(operators):
            table = high.astype(jnp.float32) + low.astype(jnp.float32)
            rows = jnp.concatenate([spectra[:, 2 * slot], spectra[:, 2 * slot + 1]], axis=-1)
            out = jnp.einsum("ncpi,ij->ncpj", rows, table, precision=precise)
            outs += [out[..., :result], out[..., result:]]
        return jnp.stack(outs, axis=1)

    panel, per_part = 256, result // 256
    group = hosts
    while group * parts * depth > 256 and group % 2 == 0:
        group //= 2
    rows = group * parts * depth

    def kernel(*refs):
        terms, in_ref, out_ref, lhs_high, lhs_low = refs[: 2 * slots], *refs[2 * slots :]

        @pl.when(pl.program_id(0) == 0)
        def _():
            for slot in range(slots):
                for part in range(2):
                    lanes = slice(part * width, (part + 1) * width)
                    value = in_ref[:, 2 * slot + part].reshape(hosts * parts * depth, width)
                    lhs_high[slot, :, lanes], lhs_low[slot, :, lanes] = split(value)

        dot = functools.partial(jnp.dot, preferred_element_type=jnp.float32)

        def multiply(index, carry):
            at = pl.ds(pl.multiple_of(index * rows, rows), rows)
            out_at = pl.ds(index * group, group)
            for slot in range(slots):
                high, low = terms[2 * slot][...], terms[2 * slot + 1][...]
                total = dot(lhs_high[slot, at, :], low) + dot(lhs_low[slot, at, :], high)
                total = total + dot(lhs_high[slot, at, :], high)
                out_ref[out_at, slot, 0] = total.reshape(group, parts, depth, panel)
            return carry

        lax.fori_loop(0, hosts // group, multiply, 0)

    shape = (hosts, slots, 2, parts, depth, result)
    out = pl.pallas_call(
        kernel,
        grid=(2 * per_part,),
        in_specs=[pl.BlockSpec((2 * width, panel), lambda t: (0, t))] * (2 * slots)
        + [pl.BlockSpec(spectra.shape, lambda t: (0, 0, 0, 0, 0))],
        out_specs=pl.BlockSpec(
            (hosts, slots, 1, parts, depth, panel),
            lambda t: (0, 0, t // per_part, 0, 0, t % per_part),
        ),
        out_shape=jax.ShapeDtypeStruct(shape, jnp.float32),
        scratch_shapes=[pltpu.VMEM((slots, hosts * parts * depth, 2 * width), jnp.bfloat16)] * 2,
        compiler_params=tile_params(1),
        cost_estimate=cost(24 * slots * hosts * parts * depth * width * result, 3 * 2**23),
    )(*[term for pair in operators for term in pair], spectra)
    return out.reshape(hosts, reals, parts, depth, result)


def upper_side(side, sides):
    return 2 * side >= sides


def routes(count, hosts, sides):
    local, slots, half = count // hosts, count // 2 // hosts, count // 2
    within = hosts // sides
    rounds = []
    for slot in range(slots):
        for turn in range(2):
            sent, direct, inside = [None] * (hosts * sides), [], []
            for g in range(sides):
                for i in range(hosts):
                    r = slots * i + slot
                    near, far = r, (count - r if r else half)
                    upper = upper_side(g, sides)
                    if upper:
                        near, far = half + r, (half - r) % half
                    is_far = (i + turn + g + upper) % 2
                    k = far if is_far else near
                    host = k // local
                    source, origin, place = host * sides + g, host // within, i
                    if is_far:
                        place = (i + hosts // 2) % hosts
                    assert sent[source] is None
                    sent[source] = k % local
                    direct.append((source, g * hosts + i))
                    inside.append((source, origin * hosts + place))
            rounds.append((sent, direct, inside))
    return rounds


def on_device(hosts, sides, activity, system, pattern, counts, background, sensitivity):
    local, frames, planes, image = activity.shape
    sino = system.shape[3]
    count = local * hosts
    slots = count // 2 // hosts
    share = planes // sides
    depth = frames * share // hosts
    device = lax.axis_index(BOTH)
    seg = lax.axis_index("seg")
    side, place = device // hosts, device % hosts
    flip = upper_side(side, sides).astype(jnp.int32)
    groups = [[g * hosts + i for i in range(hosts)] for g in range(sides)]

    def permute(array, pairs):
        return lax.ppermute(array, BOTH, pairs)

    def exchange_all(array):
        return lax.all_to_all(array, BOTH, split_axis=0, concat_axis=0, tiled=True)

    def exchange(array):
        return lax.all_to_all(
            array, BOTH, split_axis=0, concat_axis=0, tiled=True, axis_index_groups=groups
        )

    current = lax.dynamic_slice_in_dim(activity, seg * share, share, 2)
    columns = current.reshape(local, hosts, depth, image).transpose(1, 0, 2, 3)
    columns = jnp.broadcast_to(columns[None], (sides,) + columns.shape)
    columns = exchange_all(columns.reshape(sides * hosts, local, depth, image))
    columns = columns.reshape(hosts, sides, local, depth, image)

    measured = jnp.stack([counts[0].astype(jnp.float32), background[0]])
    measured = measured.reshape(2, local, frames, sides, share, sino).transpose(3, 0, 1, 2, 4, 5)
    measured = measured.reshape(sides, 2, local, hosts, depth, sino).transpose(0, 3, 1, 2, 4, 5)
    if sides == 2:
        kept = lax.dynamic_index_in_dim(measured, seg, keepdims=False)
        given = lax.dynamic_index_in_dim(measured, 1 - seg, keepdims=False)
        given = lax.ppermute(given, "seg", [(0, 1), (1, 0)])
        first = seg == 0
        measured = jnp.stack([jnp.where(first, kept, given), jnp.where(first, given, kept)])
    else:
        measured = lax.all_to_all(measured, "seg", split_axis=0, concat_axis=0, tiled=True)
    measured = measured.reshape(sides * hosts, 2, local, depth, sino)

    tables = routes(count, hosts, sides)
    masked = [
        masked_block(system, pattern, jnp.asarray(sent, jnp.int32)[device])
        for sent, _, _ in tables
    ]
    zero = slots * place + jnp.arange(slots) == 0
    if sides == 2:
        moved = []
        for turn, (_, _, inside) in enumerate(tables):
            pairs = [pair for pair in inside if pair[0] != pair[1]]
            stays = [0] * (hosts * sides)
            for source, target in inside:
                stays[target] = int(source == target)
            got = permute(masked[turn], pairs)
            moved.append(jnp.where(jnp.asarray(stays)[device] == 1, masked[turn], got))
        near, far = [], []
        for slot in range(slots):
            got = moved[2 * slot : 2 * slot + 2]
            near.append(jnp.where(seg == 0, got[0], got[1]))
            far.append(jnp.where(seg == 0, got[1], got[0]))
        across = []
        for i in range(hosts):
            other = (i + hosts // 2) % hosts
            across += [(other, hosts + i), (hosts + other, i)]
        columns, near, far = lax.optimization_barrier((columns, near, far))
        for slot in range(slots):
            far[slot] = permute(far[slot], across)
            if slot + 1 < slots:
                far[slot], far[slot + 1] = lax.optimization_barrier((far[slot], far[slot + 1]))
        far[-1], measured = lax.optimization_barrier((far[-1], measured))
        blocks = list(zip(near, far))
        odd = flip
    else:
        moved = [lax.ppermute(block, BOTH, table[1]) for block, table in zip(masked, tables)]
        blocks = [moved[2 * slot : 2 * slot + 2] for slot in range(slots)]
        odd = (place + side) % 2
    measured = exchange_all(measured).reshape(hosts, sides, 2, local, depth, sino)
    own = jnp.where(zero & (odd == 1), 0.0, 1.0)
    other = jnp.where(zero & (odd == 0), 0.0, 1.0)
    sign = jnp.where(zero, 0.0, 1.0 - 2.0 * odd)
    weights = jnp.stack([own, other, sign], axis=1)
    blocks = [(*pair, weights[slot]) for slot, pair in enumerate(blocks)]

    def by_owner(array):
        return array.reshape((hosts, 2 * slots) + array.shape[1:])

    def by_slot(array):
        return array.reshape((count,) + array.shape[2:])

    spectra = exchange(by_owner(spectrum_of(columns, flip)))
    forward = []
    for slot in range(slots):
        operator = [operator_of(*blocks[slot], False)]
        pair = apply_operators(operator, spectra[:, 2 * slot : 2 * slot + 2])
        forward.append(exchange(pair))
    forward = by_slot(jnp.concatenate(forward, axis=1))
    adjoint = [operator_of(*block, True) for block in blocks]
    spectra = exchange(by_owner(ratio_of(forward, measured, flip)))
    backward = exchange(apply_operators(adjoint, spectra))
    back = sectors_of(by_slot(backward), hosts, flip)
    back = exchange_all(back.reshape(hosts * sides, local, depth, image))
    total = back.reshape(sides, hosts, local, depth, image).sum(0).transpose(1, 0, 2, 3)
    total = total.reshape(local, frames, share, image)
    return current * total / sensitivity[:, None]


def solution(mesh):
    in_specs = (
        P("freq", None, None, None),
        P("seg", "freq", None, None, None),
        P("seg", "freq", None, None),
        P("seg", "freq", None, None, None),
        P("seg", "freq", None, None, None),
        P("freq", "seg", None),
    )
    hosts, sides = mesh.shape["freq"], mesh.shape["seg"]

    def body(activity, *rest):
        return on_device(hosts, sides, activity, *rest)

    return jax.shard_map(
        body, mesh=mesh, in_specs=in_specs, out_specs=P("freq", None, "seg", None), check_vma=False
    )
```

```python
import functools

import jax
import jax.numpy as jnp
import numpy as np
from jax import lax
from jax.experimental import pallas as pl
from jax.experimental.pallas import tpu as pltpu
from jax.sharding import PartitionSpec as P

BOTH = ("freq", "seg")
precise = lax.Precision.HIGHEST


def analyse(load, start, step, size):
    if size == 1:
        return [(load(start), None)]
    if size == 2:
        first, second = load(start), load(start + step)
        return [(first + second, None), (first - second, None)]
    even = analyse(load, start, 2 * step, size // 2)
    odd = analyse(load, start + step, 2 * step, size // 2)
    half, quarter = size // 2, size // 4
    out = [None] * (half + 1)
    out[0] = (even[0][0] + odd[0][0], None)
    out[half] = (even[0][0] - odd[0][0], None)
    out[quarter] = (even[quarter][0], -odd[quarter][0])
    for k in range(1, quarter):
        cosine, sine = float(np.cos(2 * np.pi * k / size)), float(np.sin(2 * np.pi * k / size))
        real, imag = odd[k]
        turned_real = real * cosine + imag * sine
        turned_imag = imag * cosine - real * sine
        out[k] = (even[k][0] + turned_real, even[k][1] + turned_imag)
        out[half - k] = (even[k][0] - turned_real, turned_imag - even[k][1])
    return out


def synthesise(values, emit, start, step, size):
    if size == 1:
        emit(start, values[0][0])
        return
    if size == 2:
        emit(start, values[0][0] + values[1][0])
        emit(start + step, values[0][0] - values[1][0])
        return
    half, quarter = size // 2, size // 4
    even, odd = [None] * (quarter + 1), [None] * (quarter + 1)
    even[0] = (values[0][0] + values[half][0], None)
    odd[0] = (values[0][0] - values[half][0], None)
    even[quarter] = (values[quarter][0], None)
    odd[quarter] = (-values[quarter][1], None)
    for k in range(1, quarter):
        cosine, sine = float(np.cos(2 * np.pi * k / size)), float(np.sin(2 * np.pi * k / size))
        (real, imag), (other_real, other_imag) = values[k], values[half - k]
        even[k] = (real + other_real, imag - other_imag)
        diff_real, diff_imag = real - other_real, imag + other_imag
        odd[k] = (diff_real * cosine - diff_imag * sine, diff_real * sine + diff_imag * cosine)
    synthesise(even, emit, start, 2 * step, half)
    synthesise(odd, emit, start + step, 2 * step, half)


def analysis_matrix(size):
    angles = 2 * np.pi * np.outer(np.arange(size // 2), np.arange(size)) / size
    table = np.stack([np.cos(angles), -np.sin(angles)], axis=1).reshape(size, size)
    table[1] = np.where(np.arange(size) % 2 == 0, 1.0, -1.0)
    return jnp.asarray(table, jnp.float32)


def slot_index(k, half, flip):
    return k + flip * ((half - k) % half - k)


def load_slots(ref, lanes, size, flip):
    half = size // 2
    at = [2 * slot_index(k, half, flip) for k in range(half)]
    values = [(ref[row, 0, :, lanes], ref[row + 1, 0, :, lanes]) for row in at]
    return [(values[0][0], None)] + values[1:] + [(values[0][1], None)]


def store_slots(ref, lanes, spectrum, flip):
    half = len(spectrum) - 1
    ref[0, 0, :, lanes] = spectrum[0][0]
    ref[1, 0, :, lanes] = spectrum[half][0]
    for k in range(1, half):
        row = 2 * slot_index(k, half, flip)
        ref[row, 0, :, lanes] = spectrum[k][0]
        ref[row + 1, 0, :, lanes] = spectrum[k][1]


def flipped_matrix(size, flip):
    table = analysis_matrix(size).reshape(size // 2, 2, size)
    order = slot_index(np.arange(size // 2), size // 2, flip)
    return table[order].reshape(size, size)


def each_lane_tile(width, body):
    def step(index, carry):
        body(pl.ds(pl.multiple_of(index * 128, 128), 128))
        return carry

    lax.fori_loop(0, width // 128, step, 0)


def tile_params(axes):
    return pltpu.CompilerParams(dimension_semantics=("arbitrary",) * axes)


def cost(flops, nbytes):
    return pl.CostEstimate(flops=int(flops), bytes_accessed=int(nbytes), transcendentals=0)


def slot_block(shape):
    count, _, _, width = shape
    return pl.BlockSpec((count, 1, 8, width), lambda c, t, _: (0, c, t, 0))


def sector_block(shape):
    hosts, _, local, _, width = shape
    return pl.BlockSpec((hosts, 1, local, 8, width), lambda c, t, _: (0, c, 0, t, 0))


def tiles_call(kernel, flip, parts, operands, in_specs, shape, out_spec, scratch=()):
    depth = operands[0].shape[-2]
    size = sum(operand.size for operand in operands)
    return pl.pallas_call(
        kernel,
        grid_spec=pltpu.PrefetchScalarGridSpec(
            num_scalar_prefetch=1,
            grid=(parts, depth // 8),
            in_specs=in_specs,
            out_specs=out_spec,
            scratch_shapes=scratch,
        ),
        out_shape=jax.ShapeDtypeStruct(shape, jnp.float32),
        compiler_params=tile_params(2),
        cost_estimate=cost(size * 24, size * 8),
    )(flip.reshape(1), *operands)


def spectrum_of(section, flip):
    hosts, parts, local, depth, width = section.shape
    count = hosts * local
    shape = (count, parts, depth, width)
    if depth % 8 or width % 128:
        flat = section.transpose(0, 2, 1, 3, 4).reshape(shape)
        return jnp.einsum("us,scpj->ucpj", flipped_matrix(count, flip), flat, precision=precise)

    def kernel(flip_ref, in_ref, out_ref):
        def body(lanes):
            load = lambda s: in_ref[s // local, 0, s % local, :, lanes]
            store_slots(out_ref, lanes, analyse(load, 0, 1, count), flip_ref[0])

        each_lane_tile(width, body)

    specs = [sector_block(section.shape)]
    out = slot_block(shape)
    return tiles_call(kernel, flip, parts, [section], specs, shape, out)


def sectors_of(spectrum, hosts, flip):
    count, parts, depth, width = spectrum.shape
    local = count // hosts
    shape = (hosts, parts, local, depth, width)
    if depth % 8 or width % 128:
        table = flipped_matrix(count, flip)
        flat = jnp.einsum("us,ucpj->scpj", table, spectrum, precision=precise)
        return flat.reshape(hosts, local, parts, depth, width).transpose(0, 2, 1, 3, 4)

    def kernel(flip_ref, in_ref, out_ref):
        def body(lanes):
            def emit(s, value):
                out_ref[s // local, 0, s % local, :, lanes] = value

            synthesise(load_slots(in_ref, lanes, count, flip_ref[0]), emit, 0, 1, count)

        each_lane_tile(width, body)

    specs = [slot_block(spectrum.shape)]
    out = sector_block(shape)
    return tiles_call(kernel, flip, parts, [spectrum], specs, shape, out)


def ratio_of(forward, measured, flip):
    slots = len(forward)
    owners, _, parts, depth, width = forward[0].shape
    count, half = 2 * slots * owners, slots * owners
    shape = (count, parts, depth, width)
    hosts, _, _, local = measured.shape[:4]
    scale = 1.0 / count
    if depth % 8 or width % 128 or slots > 2:
        joined = jnp.concatenate(forward, axis=1).reshape(shape)
        estimate = sectors_of(joined, hosts, flip) * scale
        expected = jnp.maximum(estimate + measured[:, :, 1], 1.0)
        return spectrum_of(measured[:, :, 0] / expected * scale, flip)

    def kernel(flip_ref, *refs):
        in_refs, measured_ref, out_ref, held = refs[:slots], *refs[slots:]

        def body(lanes):
            values = []
            for k in range(half):
                at = k // slots + flip_ref[0] * ((half - k) % half // slots - k // slots)
                ref = in_refs[k % slots]
                values.append((ref[at, 0, 0, :, lanes], ref[at, 1, 0, :, lanes]))
            values = [(values[0][0], None)] + values[1:] + [(values[0][1], None)]

            def emit(s, value):
                host, row = s // local, s % local
                expected = jnp.maximum(value * scale + measured_ref[host, 0, 1, row, :, lanes], 1.0)
                held[s] = measured_ref[host, 0, 0, row, :, lanes] / expected * scale

            synthesise(values, emit, 0, 1, count)
            spectrum = analyse(lambda s: held[s], 0, 1, count)
            store_slots(out_ref, lanes, spectrum, flip_ref[0])

        each_lane_tile(width, body)

    specs = [pl.BlockSpec((owners, 2, 1, 8, width), lambda c, t, _: (0, 0, c, t, 0))] * slots
    specs.append(pl.BlockSpec((hosts, 1, 2, local, 8, width), lambda c, t, _: (0, c, 0, 0, t, 0)))
    scratch = [pltpu.VMEM((count, 8, 128), jnp.float32)]
    out = slot_block(shape)
    return tiles_call(kernel, flip, parts, [*forward, measured], specs, shape, out, scratch)


def masked_block(system, pattern, which):
    _, _, _, height, width = system.shape
    rows, cols = pattern.shape[2:]
    tile_height, tile_width = height // rows, width // cols

    def kernel(which_ref, pattern_ref, in_ref, out_ref):
        for row in range(rows):
            for col in range(cols):
                at = (slice(row * tile_height, (row + 1) * tile_height),)
                at += (slice(col * tile_width, (col + 1) * tile_width),)
                value = pattern_ref[(which_ref[0] * rows + row) * cols + col].astype(jnp.float32)
                out_ref[(0,) + at] = in_ref[(0, 0, 0) + at] * value

    return pl.pallas_call(
        kernel,
        grid_spec=pltpu.PrefetchScalarGridSpec(
            num_scalar_prefetch=2,
            grid=(2,),
            in_specs=[pl.BlockSpec((1, 1, 1, height, width), lambda a, w, _: (0, w[0], a, 0, 0))],
            out_specs=pl.BlockSpec((1, height, width), lambda a, w, _: (a, 0, 0)),
        ),
        out_shape=jax.ShapeDtypeStruct((2, height, width), jnp.float32),
        cost_estimate=cost(2 * height * width, 16 * height * width),
        compiler_params=tile_params(1),
        name="masked",
    )(which.reshape(1), pattern.reshape(-1), system)


def split(value):
    high = value.astype(jnp.bfloat16)
    return high, (value - high.astype(jnp.float32)).astype(jnp.bfloat16)


def folded(first, second, weights):
    own, other, sign = weights[0], weights[1], weights[2]
    upper = own * first[0] + other * second[0]
    lower = other * first[0] + own * second[0]
    return upper, lower, sign * (first[1] - second[1])


def operator_of(first, second, weights, adjoint):
    height, inner = first.shape[1:]
    if height % 128 or inner % 128:
        upper, lower, cross = folded(first, second, weights)
        if adjoint:
            table = jnp.block([[upper, -cross], [cross, lower]])
        else:
            table = jnp.block([[upper.T, cross.T], [-cross.T, lower.T]])
        return split(table)
    shape = (2 * height, 2 * inner) if adjoint else (2 * inner, 2 * height)

    def kernel(weights_ref, first_ref, second_ref, high_ref, low_ref):
        def put(at, value):
            high_ref[at], low_ref[at] = split(value)

        index = pl.program_id(0)
        at = pl.ds(pl.multiple_of(index * 128, 128), 128)
        at2 = pl.ds(pl.multiple_of(index * 128 + height, 128), 128)
        upper, lower, cross = folded(first_ref, second_ref, weights_ref)
        one, two = slice(0, inner), slice(inner, 2 * inner)
        if adjoint:
            put((at, one), upper)
            put((at, two), -cross)
            put((at2, one), cross)
            put((at2, two), lower)
        else:
            cross = cross.T
            put((one, at), upper.T)
            put((one, at2), cross)
            put((two, at), -cross)
            put((two, at2), lower.T)

    return pl.pallas_call(
        kernel,
        grid_spec=pltpu.PrefetchScalarGridSpec(
            num_scalar_prefetch=1,
            grid=(height // 128,),
            in_specs=[pl.BlockSpec((2, 128, inner), lambda t, w: (0, t, 0))] * 2,
            out_specs=[pl.BlockSpec(shape, lambda t, w: (0, 0))] * 2,
        ),
        out_shape=[jax.ShapeDtypeStruct(shape, jnp.bfloat16)] * 2,
        compiler_params=tile_params(1),
        cost_estimate=cost(16 * height * inner, 32 * height * inner),
        name="operator",
    )(weights, first, second)


def apply_operators(operators, spectra, first=0):
    hosts, _, parts, depth, width = spectra.shape
    slots = len(operators)
    reals = 2 * slots
    result = operators[0][0].shape[1] // 2
    if depth % 8 or width % 128 or result % 256:
        outs = []
        for slot, (high, low) in enumerate(operators):
            table = high.astype(jnp.float32) + low.astype(jnp.float32)
            at = 2 * (first + slot)
            rows = jnp.concatenate([spectra[:, at], spectra[:, at + 1]], axis=-1)
            out = jnp.einsum("ncpi,ij->ncpj", rows, table, precision=precise)
            outs += [out[..., :result], out[..., result:]]
        return jnp.stack(outs, axis=1)

    panel, per_part = 256, result // 256
    group = hosts
    while group * parts * depth > 256 and group % 2 == 0:
        group //= 2
    rows = group * parts * depth

    def kernel(*refs):
        terms, in_ref, out_ref, lhs_high, lhs_low = refs[: 2 * slots], *refs[2 * slots :]

        @pl.when(pl.program_id(0) == 0)
        def _():
            for slot in range(slots):
                for part in range(2):
                    lanes = slice(part * width, (part + 1) * width)
                    value = in_ref[:, 2 * slot + part].reshape(hosts * parts * depth, width)
                    lhs_high[slot, :, lanes], lhs_low[slot, :, lanes] = split(value)

        dot = functools.partial(jnp.dot, preferred_element_type=jnp.float32)

        def multiply(index, carry):
            at = pl.ds(pl.multiple_of(index * rows, rows), rows)
            out_at = pl.ds(index * group, group)
            for slot in range(slots):
                high, low = terms[2 * slot][...], terms[2 * slot + 1][...]
                total = dot(lhs_high[slot, at, :], low) + dot(lhs_low[slot, at, :], high)
                total = total + dot(lhs_high[slot, at, :], high)
                out_ref[out_at, slot, 0] = total.reshape(group, parts, depth, panel)
            return carry

        lax.fori_loop(0, hosts // group, multiply, 0)

    shape = (hosts, slots, 2, parts, depth, result)
    out = pl.pallas_call(
        kernel,
        grid=(2 * per_part,),
        in_specs=[pl.BlockSpec((2 * width, panel), lambda t: (0, t))] * (2 * slots)
        + [
            pl.BlockSpec(
                (hosts, reals, parts, depth, width), lambda t: (0, first // slots, 0, 0, 0)
            )
        ],
        out_specs=pl.BlockSpec(
            (hosts, slots, 1, parts, depth, panel),
            lambda t: (0, 0, t // per_part, 0, 0, t % per_part),
        ),
        out_shape=jax.ShapeDtypeStruct(shape, jnp.float32),
        scratch_shapes=[pltpu.VMEM((slots, hosts * parts * depth, 2 * width), jnp.bfloat16)] * 2,
        compiler_params=tile_params(1),
        cost_estimate=cost(24 * slots * hosts * parts * depth * width * result, 3 * 2**23),
    )(*[term for pair in operators for term in pair], spectra)
    return out.reshape(hosts, reals, parts, depth, result)


def upper_side(side, sides):
    return 2 * side >= sides


def routes(count, hosts, sides):
    local, slots, half = count // hosts, count // 2 // hosts, count // 2
    within = hosts // sides
    rounds = []
    for slot in range(slots):
        for turn in range(2):
            sent, direct, inside = [None] * (hosts * sides), [], []
            for g in range(sides):
                for i in range(hosts):
                    r = slots * i + slot
                    near, far = r, (count - r if r else half)
                    upper = upper_side(g, sides)
                    if upper:
                        near, far = half + r, (half - r) % half
                    is_far = (i + turn + g + upper) % 2
                    k = far if is_far else near
                    host = k // local
                    source, origin, place = host * sides + g, host // within, i
                    if is_far:
                        place = (i + hosts // 2) % hosts
                    assert sent[source] is None
                    sent[source] = k % local
                    direct.append((source, g * hosts + i))
                    inside.append((source, origin * hosts + place))
            rounds.append((sent, direct, inside))
    return rounds


def on_device(hosts, sides, activity, system, pattern, counts, background, sensitivity):
    local, frames, planes, image = activity.shape
    sino = system.shape[3]
    count = local * hosts
    slots = count // 2 // hosts
    share = planes // sides
    depth = frames * share // hosts
    device = lax.axis_index(BOTH)
    seg = lax.axis_index("seg")
    side, place = device // hosts, device % hosts
    flip = upper_side(side, sides).astype(jnp.int32)
    groups = [[g * hosts + i for i in range(hosts)] for g in range(sides)]

    def permute(array, pairs):
        return lax.ppermute(array, BOTH, pairs)

    def exchange_all(array):
        return lax.all_to_all(array, BOTH, split_axis=0, concat_axis=0, tiled=True)

    def exchange(array):
        return lax.all_to_all(
            array, BOTH, split_axis=0, concat_axis=0, tiled=True, axis_index_groups=groups
        )

    current = lax.dynamic_slice_in_dim(activity, seg * share, share, 2)
    columns = current.reshape(local, hosts, depth, image).transpose(1, 0, 2, 3)
    columns = jnp.broadcast_to(columns[None], (sides,) + columns.shape)
    columns = exchange_all(columns.reshape(sides * hosts, local, depth, image))
    columns = columns.reshape(hosts, sides, local, depth, image)

    measured = jnp.stack([counts[0].astype(jnp.float32), background[0]])
    measured = measured.reshape(2, local, frames, sides, share, sino).transpose(3, 0, 1, 2, 4, 5)
    measured = measured.reshape(sides, 2, local, hosts, depth, sino).transpose(0, 3, 1, 2, 4, 5)
    if sides == 2:
        kept = lax.dynamic_index_in_dim(measured, seg, keepdims=False)
        given = lax.dynamic_index_in_dim(measured, 1 - seg, keepdims=False)
        given = lax.ppermute(given, "seg", [(0, 1), (1, 0)])
        first = seg == 0
        measured = jnp.stack([jnp.where(first, kept, given), jnp.where(first, given, kept)])
    else:
        measured = lax.all_to_all(measured, "seg", split_axis=0, concat_axis=0, tiled=True)
    measured = measured.reshape(sides * hosts, 2, local, depth, sino)

    tables = routes(count, hosts, sides)
    masked = [
        masked_block(system, pattern, jnp.asarray(sent, jnp.int32)[device])
        for sent, _, _ in tables
    ]
    zero = slots * place + jnp.arange(slots) == 0
    if sides == 2:
        moved = []
        for turn, (_, _, inside) in enumerate(tables):
            pairs = [pair for pair in inside if pair[0] != pair[1]]
            stays = [0] * (hosts * sides)
            for source, target in inside:
                stays[target] = int(source == target)
            got = permute(masked[turn], pairs)
            moved.append(jnp.where(jnp.asarray(stays)[device] == 1, masked[turn], got))
        near, far = [], []
        for slot in range(slots):
            got = moved[2 * slot : 2 * slot + 2]
            near.append(jnp.where(seg == 0, got[0], got[1]))
            far.append(jnp.where(seg == 0, got[1], got[0]))
        across = []
        for i in range(hosts):
            other = (i + hosts // 2) % hosts
            across += [(other, hosts + i), (hosts + other, i)]
        for slot in range(slots):
            far[slot] = permute(far[slot], across)
            if slot + 1 < slots:
                far[slot], far[slot + 1] = lax.optimization_barrier((far[slot], far[slot + 1]))
        far[-1], measured = lax.optimization_barrier((far[-1], measured))
        blocks = list(zip(near, far))
        odd = flip
    else:
        moved = [lax.ppermute(block, BOTH, table[1]) for block, table in zip(masked, tables)]
        blocks = [moved[2 * slot : 2 * slot + 2] for slot in range(slots)]
        odd = (place + side) % 2
    measured = exchange_all(measured).reshape(hosts, sides, 2, local, depth, sino)
    own = jnp.where(zero & (odd == 1), 0.0, 1.0)
    other = jnp.where(zero & (odd == 0), 0.0, 1.0)
    sign = jnp.where(zero, 0.0, 1.0 - 2.0 * odd)
    weights = jnp.stack([own, other, sign], axis=1)
    blocks = [(*pair, weights[slot]) for slot, pair in enumerate(blocks)]

    def by_owner(array):
        return array.reshape((hosts, 2 * slots) + array.shape[1:])

    def by_slot(array):
        return array.reshape((count,) + array.shape[2:])

    spectra = by_owner(spectrum_of(columns, flip))
    spectra = exchange(spectra)
    forward = []
    for slot in range(slots):
        operator = [operator_of(*blocks[slot], False)]
        pair = apply_operators(operator, spectra, slot)
        forward.append(exchange(pair))
    adjoint = [operator_of(*block, True) for block in blocks]
    spectra = exchange(by_owner(ratio_of(forward, measured, flip)))
    backward = exchange(apply_operators(adjoint, spectra))
    back = sectors_of(by_slot(backward), hosts, flip)
    back = exchange_all(back.reshape(hosts * sides, local, depth, image))
    total = back.reshape(sides, hosts, local, depth, image).sum(0).transpose(1, 0, 2, 3)
    total = total.reshape(local, frames, share, image)
    return current * total / sensitivity[:, None]


def solution(mesh):
    in_specs = (
        P("freq", None, None, None),
        P("seg", "freq", None, None, None),
        P("seg", "freq", None, None),
        P("seg", "freq", None, None, None),
        P("seg", "freq", None, None, None),
        P("freq", "seg", None),
    )
    hosts, sides = mesh.shape["freq"], mesh.shape["seg"]

    def body(activity, *rest):
        return on_device(hosts, sides, activity, *rest)

    return jax.shard_map(
        body, mesh=mesh, in_specs=in_specs, out_specs=P("freq", None, "seg", None), check_vma=False
    )
```

```python
import functools

import jax
import jax.numpy as jnp
import numpy as np
from jax import lax
from jax.experimental import pallas as pl
from jax.experimental.pallas import tpu as pltpu
from jax.sharding import PartitionSpec as P

BOTH = ("freq", "seg")
precise = lax.Precision.HIGHEST


def analyse(load, start, step, size):
    if size == 1:
        return [(load(start), None)]
    if size == 2:
        first, second = load(start), load(start + step)
        return [(first + second, None), (first - second, None)]
    even = analyse(load, start, 2 * step, size // 2)
    odd = analyse(load, start + step, 2 * step, size // 2)
    half, quarter = size // 2, size // 4
    out = [None] * (half + 1)
    out[0] = (even[0][0] + odd[0][0], None)
    out[half] = (even[0][0] - odd[0][0], None)
    out[quarter] = (even[quarter][0], -odd[quarter][0])
    for k in range(1, quarter):
        cosine, sine = float(np.cos(2 * np.pi * k / size)), float(np.sin(2 * np.pi * k / size))
        real, imag = odd[k]
        turned_real = real * cosine + imag * sine
        turned_imag = imag * cosine - real * sine
        out[k] = (even[k][0] + turned_real, even[k][1] + turned_imag)
        out[half - k] = (even[k][0] - turned_real, turned_imag - even[k][1])
    return out


def synthesise(values, emit, start, step, size):
    if size == 1:
        emit(start, values[0][0])
        return
    if size == 2:
        emit(start, values[0][0] + values[1][0])
        emit(start + step, values[0][0] - values[1][0])
        return
    half, quarter = size // 2, size // 4
    even, odd = [None] * (quarter + 1), [None] * (quarter + 1)
    even[0] = (values[0][0] + values[half][0], None)
    odd[0] = (values[0][0] - values[half][0], None)
    even[quarter] = (values[quarter][0], None)
    odd[quarter] = (-values[quarter][1], None)
    for k in range(1, quarter):
        cosine, sine = float(np.cos(2 * np.pi * k / size)), float(np.sin(2 * np.pi * k / size))
        (real, imag), (other_real, other_imag) = values[k], values[half - k]
        even[k] = (real + other_real, imag - other_imag)
        diff_real, diff_imag = real - other_real, imag + other_imag
        odd[k] = (diff_real * cosine - diff_imag * sine, diff_real * sine + diff_imag * cosine)
    synthesise(even, emit, start, 2 * step, half)
    synthesise(odd, emit, start + step, 2 * step, half)


def analysis_matrix(size):
    angles = 2 * np.pi * np.outer(np.arange(size // 2), np.arange(size)) / size
    table = np.stack([np.cos(angles), -np.sin(angles)], axis=1).reshape(size, size)
    table[1] = np.where(np.arange(size) % 2 == 0, 1.0, -1.0)
    return jnp.asarray(table, jnp.float32)


def slot_index(k, half, flip):
    return k + flip * ((half - k) % half - k)


def load_slots(ref, lanes, size, flip):
    half = size // 2
    at = [2 * slot_index(k, half, flip) for k in range(half)]
    values = [(ref[row, 0, :, lanes], ref[row + 1, 0, :, lanes]) for row in at]
    return [(values[0][0], None)] + values[1:] + [(values[0][1], None)]


def store_slots(ref, lanes, spectrum, flip):
    half = len(spectrum) - 1
    ref[0, 0, :, lanes] = spectrum[0][0]
    ref[1, 0, :, lanes] = spectrum[half][0]
    for k in range(1, half):
        row = 2 * slot_index(k, half, flip)
        ref[row, 0, :, lanes] = spectrum[k][0]
        ref[row + 1, 0, :, lanes] = spectrum[k][1]


def flipped_matrix(size, flip):
    table = analysis_matrix(size).reshape(size // 2, 2, size)
    order = slot_index(np.arange(size // 2), size // 2, flip)
    return table[order].reshape(size, size)


def each_lane_tile(width, body):
    def step(index, carry):
        body(pl.ds(pl.multiple_of(index * 128, 128), 128))
        return carry

    lax.fori_loop(0, width // 128, step, 0)


def tile_params(axes):
    return pltpu.CompilerParams(dimension_semantics=("arbitrary",) * axes)


def cost(flops, nbytes):
    return pl.CostEstimate(flops=int(flops), bytes_accessed=int(nbytes), transcendentals=0)


def slot_block(shape):
    count, _, _, width = shape
    return pl.BlockSpec((count, 1, 8, width), lambda c, t, _: (0, c, t, 0))


def sector_block(shape):
    hosts, _, local, _, width = shape
    return pl.BlockSpec((hosts, 1, local, 8, width), lambda c, t, _: (0, c, 0, t, 0))


def tiles_call(kernel, flip, parts, operands, in_specs, shape, out_spec, scratch=()):
    depth = operands[0].shape[-2]
    size = sum(operand.size for operand in operands)
    return pl.pallas_call(
        kernel,
        grid_spec=pltpu.PrefetchScalarGridSpec(
            num_scalar_prefetch=1,
            grid=(parts, depth // 8),
            in_specs=in_specs,
            out_specs=out_spec,
            scratch_shapes=scratch,
        ),
        out_shape=jax.ShapeDtypeStruct(shape, jnp.float32),
        compiler_params=tile_params(2),
        cost_estimate=cost(size * 24, size * 8),
    )(flip.reshape(-1), *operands)


def spectrum_of(section, flip):
    hosts, parts, local, depth, width = section.shape
    count = hosts * local
    shape = (count, parts, depth, width)
    if depth % 8 or width % 128:
        flat = section.transpose(0, 2, 1, 3, 4).reshape(shape)
        return jnp.einsum("us,scpj->ucpj", flipped_matrix(count, flip), flat, precision=precise)

    def kernel(flip_ref, in_ref, out_ref):
        def body(lanes):
            load = lambda s: in_ref[s // local, 0, s % local, :, lanes]
            store_slots(out_ref, lanes, analyse(load, 0, 1, count), flip_ref[0])

        each_lane_tile(width, body)

    specs = [sector_block(section.shape)]
    out = slot_block(shape)
    return tiles_call(kernel, flip, parts, [section], specs, shape, out)


def sectors_of(spectrum, hosts, flip):
    count, parts, depth, width = spectrum.shape
    local = count // hosts
    shape = (hosts, parts, local, depth, width)
    if depth % 8 or width % 128:
        table = flipped_matrix(count, flip)
        flat = jnp.einsum("us,ucpj->scpj", table, spectrum, precision=precise)
        return flat.reshape(hosts, local, parts, depth, width).transpose(0, 2, 1, 3, 4)

    def kernel(flip_ref, in_ref, out_ref):
        def body(lanes):
            def emit(s, value):
                out_ref[s // local, 0, s % local, :, lanes] = value

            synthesise(load_slots(in_ref, lanes, count, flip_ref[0]), emit, 0, 1, count)

        each_lane_tile(width, body)

    specs = [slot_block(spectrum.shape)]
    out = sector_block(shape)
    return tiles_call(kernel, flip, parts, [spectrum], specs, shape, out)


def ratio_of(pieces, place, measured, flip):
    owners = len(pieces)
    reals, parts, depth, width = pieces[0].shape
    count, half = reals * owners, reals * owners // 2
    shape = (count, parts, depth, width)
    hosts, _, _, local = measured.shape[:4]
    scale = 1.0 / count
    if depth % 8 or width % 128:
        joined = jnp.stack(pieces)[(place - np.arange(owners)) % owners].reshape(shape)
        estimate = sectors_of(joined, hosts, flip) * scale
        expected = jnp.maximum(estimate + measured[:, :, 1], 1.0)
        return spectrum_of(measured[:, :, 0] / expected * scale, flip)

    def kernel(flip_ref, *refs):
        in_refs, measured_ref, out_ref, held = refs[:owners], *refs[owners:]

        def body(lanes):
            for j in range(owners):
                at = lax.rem(flip_ref[1] + (owners - j), owners) * reals
                for u in range(reals):
                    held[at + u] = in_refs[j][u, 0, :, lanes]
            values = []
            for k in range(half):
                row = 2 * slot_index(k, half, flip_ref[0])
                values.append((held[row], held[row + 1]))
            values = [(values[0][0], None)] + values[1:] + [(values[0][1], None)]

            def emit(s, value):
                host, row = s // local, s % local
                expected = jnp.maximum(value * scale + measured_ref[host, 0, 1, row, :, lanes], 1.0)
                held[s] = measured_ref[host, 0, 0, row, :, lanes] / expected * scale

            synthesise(values, emit, 0, 1, count)
            spectrum = analyse(lambda s: held[s], 0, 1, count)
            store_slots(out_ref, lanes, spectrum, flip_ref[0])

        each_lane_tile(width, body)

    specs = [pl.BlockSpec((reals, 1, 8, width), lambda c, t, _: (0, c, t, 0))] * owners
    specs.append(pl.BlockSpec((hosts, 1, 2, local, 8, width), lambda c, t, _: (0, c, 0, 0, t, 0)))
    scratch = [pltpu.VMEM((count, 8, 128), jnp.float32)]
    return tiles_call(
        kernel,
        jnp.stack([flip, place]),
        parts,
        [*pieces, measured],
        specs,
        shape,
        slot_block(shape),
        scratch,
    )


def masked_block(system, pattern, which):
    _, _, _, height, width = system.shape
    rows, cols = pattern.shape[2:]
    tile_height, tile_width = height // rows, width // cols

    def kernel(which_ref, pattern_ref, in_ref, out_ref):
        for row in range(rows):
            for col in range(cols):
                at = (slice(row * tile_height, (row + 1) * tile_height),)
                at += (slice(col * tile_width, (col + 1) * tile_width),)
                value = pattern_ref[(which_ref[0] * rows + row) * cols + col].astype(jnp.float32)
                out_ref[(0,) + at] = in_ref[(0, 0, 0) + at] * value

    return pl.pallas_call(
        kernel,
        grid_spec=pltpu.PrefetchScalarGridSpec(
            num_scalar_prefetch=2,
            grid=(2,),
            in_specs=[pl.BlockSpec((1, 1, 1, height, width), lambda a, w, _: (0, w[0], a, 0, 0))],
            out_specs=pl.BlockSpec((1, height, width), lambda a, w, _: (a, 0, 0)),
        ),
        out_shape=jax.ShapeDtypeStruct((2, height, width), jnp.float32),
        cost_estimate=cost(2 * height * width, 16 * height * width),
        compiler_params=tile_params(1),
        name="masked",
    )(which.reshape(1), pattern.reshape(-1), system)


def split(value):
    high = value.astype(jnp.bfloat16)
    return high, (value - high.astype(jnp.float32)).astype(jnp.bfloat16)


def folded(first, second, weights):
    own, other, sign = weights[0], weights[1], weights[2]
    upper = own * first[0] + other * second[0]
    lower = other * first[0] + own * second[0]
    return upper, lower, sign * (first[1] - second[1])


def operator_of(first, second, weights, adjoint):
    height, inner = first.shape[1:]
    if height % 128 or inner % 128:
        upper, lower, cross = folded(first, second, weights)
        if adjoint:
            table = jnp.block([[upper, -cross], [cross, lower]])
        else:
            table = jnp.block([[upper.T, cross.T], [-cross.T, lower.T]])
        return split(table)
    shape = (2 * height, 2 * inner) if adjoint else (2 * inner, 2 * height)

    def kernel(weights_ref, first_ref, second_ref, high_ref, low_ref):
        def put(at, value):
            high_ref[at], low_ref[at] = split(value)

        index = pl.program_id(0)
        at = pl.ds(pl.multiple_of(index * 128, 128), 128)
        at2 = pl.ds(pl.multiple_of(index * 128 + height, 128), 128)
        upper, lower, cross = folded(first_ref, second_ref, weights_ref)
        one, two = slice(0, inner), slice(inner, 2 * inner)
        if adjoint:
            put((at, one), upper)
            put((at, two), -cross)
            put((at2, one), cross)
            put((at2, two), lower)
        else:
            cross = cross.T
            put((one, at), upper.T)
            put((one, at2), cross)
            put((two, at), -cross)
            put((two, at2), lower.T)

    return pl.pallas_call(
        kernel,
        grid_spec=pltpu.PrefetchScalarGridSpec(
            num_scalar_prefetch=1,
            grid=(height // 128,),
            in_specs=[pl.BlockSpec((2, 128, inner), lambda t, w: (0, t, 0))] * 2,
            out_specs=[pl.BlockSpec(shape, lambda t, w: (0, 0))] * 2,
        ),
        out_shape=[jax.ShapeDtypeStruct(shape, jnp.bfloat16)] * 2,
        compiler_params=tile_params(1),
        cost_estimate=cost(16 * height * inner, 32 * height * inner),
        name="operator",
    )(weights, first, second)


def apply_operators(operators, spectra, first=0):
    hosts, _, parts, depth, width = spectra.shape
    slots = len(operators)
    reals = 2 * slots
    result = operators[0][0].shape[1] // 2
    if depth % 8 or width % 128 or result % 256:
        outs = []
        for slot, (high, low) in enumerate(operators):
            table = high.astype(jnp.float32) + low.astype(jnp.float32)
            at = 2 * (first + slot)
            rows = jnp.concatenate([spectra[:, at], spectra[:, at + 1]], axis=-1)
            out = jnp.einsum("ncpi,ij->ncpj", rows, table, precision=precise)
            outs += [out[..., :result], out[..., result:]]
        return jnp.stack(outs, axis=1)

    panel, per_part = 256, result // 256
    group = hosts
    while group * parts * depth > 256 and group % 2 == 0:
        group //= 2
    rows = group * parts * depth

    def kernel(*refs):
        terms, in_ref, out_ref, lhs_high, lhs_low = refs[: 2 * slots], *refs[2 * slots :]

        @pl.when(pl.program_id(0) == 0)
        def _():
            for slot in range(slots):
                for part in range(2):
                    lanes = slice(part * width, (part + 1) * width)
                    value = in_ref[:, 2 * slot + part].reshape(hosts * parts * depth, width)
                    lhs_high[slot, :, lanes], lhs_low[slot, :, lanes] = split(value)

        dot = functools.partial(jnp.dot, preferred_element_type=jnp.float32)

        def multiply(index, carry):
            at = pl.ds(pl.multiple_of(index * rows, rows), rows)
            out_at = pl.ds(index * group, group)
            for slot in range(slots):
                high, low = terms[2 * slot][...], terms[2 * slot + 1][...]
                total = dot(lhs_high[slot, at, :], low) + dot(lhs_low[slot, at, :], high)
                total = total + dot(lhs_high[slot, at, :], high)
                out_ref[out_at, slot, 0] = total.reshape(group, parts, depth, panel)
            return carry

        lax.fori_loop(0, hosts // group, multiply, 0)

    shape = (hosts, slots, 2, parts, depth, result)
    out = pl.pallas_call(
        kernel,
        grid=(2 * per_part,),
        in_specs=[pl.BlockSpec((2 * width, panel), lambda t: (0, t))] * (2 * slots)
        + [
            pl.BlockSpec(
                (hosts, reals, parts, depth, width), lambda t: (0, first // slots, 0, 0, 0)
            )
        ],
        out_specs=pl.BlockSpec(
            (hosts, slots, 1, parts, depth, panel),
            lambda t: (0, 0, t // per_part, 0, 0, t % per_part),
        ),
        out_shape=jax.ShapeDtypeStruct(shape, jnp.float32),
        scratch_shapes=[pltpu.VMEM((slots, hosts * parts * depth, 2 * width), jnp.bfloat16)] * 2,
        compiler_params=tile_params(1),
        cost_estimate=cost(24 * slots * hosts * parts * depth * width * result, 3 * 2**23),
    )(*[term for pair in operators for term in pair], spectra)
    return out.reshape(hosts, reals, parts, depth, result)


def upper_side(side, sides):
    return 2 * side >= sides


def routes(count, hosts, sides):
    local, slots, half = count // hosts, count // 2 // hosts, count // 2
    within = hosts // sides
    rounds = []
    for slot in range(slots):
        for turn in range(2):
            sent, direct, inside = [None] * (hosts * sides), [], []
            for g in range(sides):
                for i in range(hosts):
                    r = slots * i + slot
                    near, far = r, (count - r if r else half)
                    upper = upper_side(g, sides)
                    if upper:
                        near, far = half + r, (half - r) % half
                    is_far = (i + turn + g + upper) % 2
                    k = far if is_far else near
                    host = k // local
                    source, origin, place = host * sides + g, host // within, i
                    if is_far:
                        place = (i + hosts // 2) % hosts
                    assert sent[source] is None
                    sent[source] = k % local
                    direct.append((source, g * hosts + i))
                    inside.append((source, origin * hosts + place))
            rounds.append((sent, direct, inside))
    return rounds


def on_device(hosts, sides, activity, system, pattern, counts, background, sensitivity):
    local, frames, planes, image = activity.shape
    sino = system.shape[3]
    count = local * hosts
    slots = count // 2 // hosts
    share = planes // sides
    depth = frames * share // hosts
    device = lax.axis_index(BOTH)
    seg = lax.axis_index("seg")
    side, place = device // hosts, device % hosts
    flip = upper_side(side, sides).astype(jnp.int32)
    groups = [[g * hosts + i for i in range(hosts)] for g in range(sides)]

    def permute(array, pairs):
        return lax.ppermute(array, BOTH, pairs)

    def exchange_all(array):
        return lax.all_to_all(array, BOTH, split_axis=0, concat_axis=0, tiled=True)

    def exchange(array):
        return lax.all_to_all(
            array, BOTH, split_axis=0, concat_axis=0, tiled=True, axis_index_groups=groups
        )

    current = lax.dynamic_slice_in_dim(activity, seg * share, share, 2)
    columns = current.reshape(local, hosts, depth, image).transpose(1, 0, 2, 3)
    columns = jnp.broadcast_to(columns[None], (sides,) + columns.shape)
    columns = exchange_all(columns.reshape(sides * hosts, local, depth, image))
    columns = columns.reshape(hosts, sides, local, depth, image)

    measured = jnp.stack([counts[0].astype(jnp.float32), background[0]])
    measured = measured.reshape(2, local, frames, sides, share, sino).transpose(3, 0, 1, 2, 4, 5)
    measured = measured.reshape(sides, 2, local, hosts, depth, sino).transpose(0, 3, 1, 2, 4, 5)
    if sides == 2:
        kept = lax.dynamic_index_in_dim(measured, seg, keepdims=False)
        given = lax.dynamic_index_in_dim(measured, 1 - seg, keepdims=False)
        given = lax.ppermute(given, "seg", [(0, 1), (1, 0)])
        first = seg == 0
        measured = jnp.stack([jnp.where(first, kept, given), jnp.where(first, given, kept)])
    else:
        measured = lax.all_to_all(measured, "seg", split_axis=0, concat_axis=0, tiled=True)
    measured = measured.reshape(sides * hosts, 2, local, depth, sino)

    tables = routes(count, hosts, sides)
    masked = [
        masked_block(system, pattern, jnp.asarray(sent, jnp.int32)[device])
        for sent, _, _ in tables
    ]
    zero = slots * place + jnp.arange(slots) == 0
    if sides == 2:
        moved = []
        for turn, (_, _, inside) in enumerate(tables):
            pairs = [pair for pair in inside if pair[0] != pair[1]]
            stays = [0] * (hosts * sides)
            for source, target in inside:
                stays[target] = int(source == target)
            got = permute(masked[turn], pairs)
            moved.append(jnp.where(jnp.asarray(stays)[device] == 1, masked[turn], got))
        near, far = [], []
        for slot in range(slots):
            got = moved[2 * slot : 2 * slot + 2]
            near.append(jnp.where(seg == 0, got[0], got[1]))
            far.append(jnp.where(seg == 0, got[1], got[0]))
        across = []
        for i in range(hosts):
            other = (i + hosts // 2) % hosts
            across += [(other, hosts + i), (hosts + other, i)]
        far = [permute(block, across) for block in far]
        far, measured = lax.optimization_barrier((far, measured))
        blocks = list(zip(near, far))
        odd = flip
    else:
        moved = [lax.ppermute(block, BOTH, table[1]) for block, table in zip(masked, tables)]
        blocks = [moved[2 * slot : 2 * slot + 2] for slot in range(slots)]
        odd = (place + side) % 2
    measured = exchange_all(measured).reshape(hosts, sides, 2, local, depth, sino)
    own = jnp.where(zero & (odd == 1), 0.0, 1.0)
    other = jnp.where(zero & (odd == 0), 0.0, 1.0)
    sign = jnp.where(zero, 0.0, 1.0 - 2.0 * odd)
    weights = jnp.stack([own, other, sign], axis=1)
    blocks = [(*pair, weights[slot]) for slot, pair in enumerate(blocks)]

    def by_owner(array):
        return array.reshape((hosts, 2 * slots) + array.shape[1:])

    def by_slot(array):
        return array.reshape((count,) + array.shape[2:])

    spectra = by_owner(spectrum_of(columns, flip))
    spectra = exchange(spectra)
    project = [operator_of(*block, False) for block in blocks]
    forward = apply_operators(project, spectra)
    pieces = []
    for j in range(hosts):
        piece = lax.dynamic_index_in_dim(forward, (place + j) % hosts, keepdims=False)
        if j:
            pairs = [(a, a // hosts * hosts + (a + j) % hosts) for a in range(sides * hosts)]
            piece = permute(piece, pairs)
        pieces.append(piece)
    adjoint = [operator_of(*block, True) for block in blocks]
    spectra = exchange(by_owner(ratio_of(pieces, place, measured, flip)))
    backward = exchange(apply_operators(adjoint, spectra))
    back = sectors_of(by_slot(backward), hosts, flip)
    back = exchange_all(back.reshape(hosts * sides, local, depth, image))
    total = back.reshape(sides, hosts, local, depth, image).sum(0).transpose(1, 0, 2, 3)
    total = total.reshape(local, frames, share, image)
    return current * total / sensitivity[:, None]


def solution(mesh):
    in_specs = (
        P("freq", None, None, None),
        P("seg", "freq", None, None, None),
        P("seg", "freq", None, None),
        P("seg", "freq", None, None, None),
        P("seg", "freq", None, None, None),
        P("freq", "seg", None),
    )
    hosts, sides = mesh.shape["freq"], mesh.shape["seg"]

    def body(activity, *rest):
        return on_device(hosts, sides, activity, *rest)

    return jax.shard_map(
        body, mesh=mesh, in_specs=in_specs, out_specs=P("freq", None, "seg", None), check_vma=False
    )
```

```python
import functools

import jax
import jax.numpy as jnp
import numpy as np
from jax import lax
from jax.experimental import pallas as pl
from jax.experimental.pallas import tpu as pltpu
from jax.sharding import PartitionSpec as P

BOTH = ("freq", "seg")
precise = lax.Precision.HIGHEST


def analyse(load, start, step, size):
    if size == 1:
        return [(load(start), None)]
    if size == 2:
        first, second = load(start), load(start + step)
        return [(first + second, None), (first - second, None)]
    even = analyse(load, start, 2 * step, size // 2)
    odd = analyse(load, start + step, 2 * step, size // 2)
    half, quarter = size // 2, size // 4
    out = [None] * (half + 1)
    out[0] = (even[0][0] + odd[0][0], None)
    out[half] = (even[0][0] - odd[0][0], None)
    out[quarter] = (even[quarter][0], -odd[quarter][0])
    for k in range(1, quarter):
        cosine, sine = float(np.cos(2 * np.pi * k / size)), float(np.sin(2 * np.pi * k / size))
        real, imag = odd[k]
        turned_real = real * cosine + imag * sine
        turned_imag = imag * cosine - real * sine
        out[k] = (even[k][0] + turned_real, even[k][1] + turned_imag)
        out[half - k] = (even[k][0] - turned_real, turned_imag - even[k][1])
    return out


def synthesise(values, emit, start, step, size):
    if size == 1:
        emit(start, values[0][0])
        return
    if size == 2:
        emit(start, values[0][0] + values[1][0])
        emit(start + step, values[0][0] - values[1][0])
        return
    half, quarter = size // 2, size // 4
    even, odd = [None] * (quarter + 1), [None] * (quarter + 1)
    even[0] = (values[0][0] + values[half][0], None)
    odd[0] = (values[0][0] - values[half][0], None)
    even[quarter] = (values[quarter][0], None)
    odd[quarter] = (-values[quarter][1], None)
    for k in range(1, quarter):
        cosine, sine = float(np.cos(2 * np.pi * k / size)), float(np.sin(2 * np.pi * k / size))
        (real, imag), (other_real, other_imag) = values[k], values[half - k]
        even[k] = (real + other_real, imag - other_imag)
        diff_real, diff_imag = real - other_real, imag + other_imag
        odd[k] = (diff_real * cosine - diff_imag * sine, diff_real * sine + diff_imag * cosine)
    synthesise(even, emit, start, 2 * step, half)
    synthesise(odd, emit, start + step, 2 * step, half)


def analysis_matrix(size):
    angles = 2 * np.pi * np.outer(np.arange(size // 2), np.arange(size)) / size
    table = np.stack([np.cos(angles), -np.sin(angles)], axis=1).reshape(size, size)
    table[1] = np.where(np.arange(size) % 2 == 0, 1.0, -1.0)
    return jnp.asarray(table, jnp.float32)


def slot_index(k, half, flip):
    return k + flip * ((half - k) % half - k)


def load_slots(held, size, flip):
    half = size // 2
    at = [2 * slot_index(k, half, flip) for k in range(half)]
    values = [(held[row], held[row + 1]) for row in at]
    return [(values[0][0], None)] + values[1:] + [(values[0][1], None)]


def store_slots(held, spectrum, flip):
    half = len(spectrum) - 1
    held[0] = spectrum[0][0]
    held[1] = spectrum[half][0]
    for k in range(1, half):
        row = 2 * slot_index(k, half, flip)
        held[row] = spectrum[k][0]
        held[row + 1] = spectrum[k][1]


def flipped_matrix(size, flip):
    table = analysis_matrix(size).reshape(size // 2, 2, size)
    order = slot_index(np.arange(size // 2), size // 2, flip)
    return table[order].reshape(size, size)


def each_lane_tile(width, body):
    def step(index, carry):
        body(pl.ds(pl.multiple_of(index * 128, 128), 128))
        return carry

    lax.fori_loop(0, width // 128, step, 0)


def tile_params(axes):
    return pltpu.CompilerParams(dimension_semantics=("arbitrary",) * axes)


def cost(flops, nbytes):
    return pl.CostEstimate(flops=int(flops), bytes_accessed=int(nbytes), transcendentals=0)


def gather_pieces(refs, held, place, lanes):
    reals = refs[0].shape[0]
    for j, ref in enumerate(refs):
        at = lax.rem(place + j, len(refs)) * reals
        for u in range(reals):
            held[at + u] = ref[u, 0, :, lanes]


def scatter_pieces(refs, held, place, lanes):
    reals = refs[0].shape[0]
    for j, ref in enumerate(refs):
        at = lax.rem(place + j, len(refs)) * reals
        for u in range(reals):
            ref[u, 0, :, lanes] = held[at + u]


def joined(pieces, place):
    owners = len(pieces)
    array = jnp.stack(pieces)[(np.arange(owners) - place) % owners]
    return array.reshape((owners * pieces[0].shape[0],) + pieces[0].shape[1:])


def parted(array, owners, place):
    array = array.reshape((owners, array.shape[0] // owners) + array.shape[1:])
    return [
        lax.dynamic_index_in_dim(array, (place + j) % owners, keepdims=False)
        for j in range(owners)
    ]


def piece_block(shape, offset=0):
    reals, _, _, width = shape
    return pl.BlockSpec((reals, 1, 8, width), lambda c, t, _: (0, c, t + offset, 0))


def sector_block(shape):
    hosts, _, local, _, width = shape
    return pl.BlockSpec((hosts, 1, local, 8, width), lambda c, t, _: (0, c, 0, t, 0))


def tiles_call(kernel, scalars, grid, operands, in_specs, shapes, out_specs, count):
    size = sum(operand.size for operand in operands)
    return pl.pallas_call(
        kernel,
        grid_spec=pltpu.PrefetchScalarGridSpec(
            num_scalar_prefetch=1,
            grid=grid,
            in_specs=in_specs,
            out_specs=out_specs,
            scratch_shapes=[pltpu.VMEM((count, 8, 128), jnp.float32)],
        ),
        out_shape=[jax.ShapeDtypeStruct(shape, jnp.float32) for shape in shapes],
        compiler_params=tile_params(2),
        cost_estimate=cost(size * 24, size * 8),
    )(jnp.stack(scalars), *operands)


def spectrum_of(section, owners, place, flip):
    hosts, parts, local, depth, width = section.shape
    count = hosts * local
    if depth % 8 or width % 128:
        flat = section.transpose(0, 2, 1, 3, 4).reshape(count, parts, depth, width)
        flat = jnp.einsum("us,scpj->ucpj", flipped_matrix(count, flip), flat, precision=precise)
        return parted(flat, owners, place)

    def kernel(scalars, in_ref, *refs):
        out_refs, held = refs[:owners], refs[owners]

        def body(lanes):
            load = lambda s: in_ref[s // local, 0, s % local, :, lanes]
            store_slots(held, analyse(load, 0, 1, count), scalars[0])
            scatter_pieces(out_refs, held, scalars[1], lanes)

        each_lane_tile(width, body)

    shape = (count // owners, parts, depth, width)
    return tiles_call(
        kernel,
        [flip, place],
        (parts, depth // 8),
        [section],
        [sector_block(section.shape)],
        [shape] * owners,
        [piece_block(shape)] * owners,
        count,
    )


def sectors_of(pieces, hosts, place, flip):
    owners = len(pieces)
    reals, parts, depth, width = pieces[0].shape
    count = owners * reals
    local = count // hosts
    shape = (hosts, parts, local, depth, width)
    if depth % 8 or width % 128:
        table = flipped_matrix(count, flip)
        flat = jnp.einsum("us,ucpj->scpj", table, joined(pieces, place), precision=precise)
        return flat.reshape(hosts, local, parts, depth, width).transpose(0, 2, 1, 3, 4)

    def kernel(scalars, *refs):
        in_refs, out_ref, held = refs[:owners], *refs[owners:]

        def body(lanes):
            def emit(s, value):
                out_ref[s // local, 0, s % local, :, lanes] = value

            gather_pieces(in_refs, held, scalars[1], lanes)
            synthesise(load_slots(held, count, scalars[0]), emit, 0, 1, count)

        each_lane_tile(width, body)

    return tiles_call(
        kernel,
        [flip, place],
        (parts, depth // 8),
        pieces,
        [piece_block(pieces[0].shape)] * owners,
        [shape],
        [sector_block(shape)],
        count,
    )[0]


def ratio_of(pieces, measured, start, place, flip):
    owners = len(pieces)
    reals, parts, _, width = pieces[0].shape
    count = owners * reals
    hosts, _, _, local, depth, _ = measured.shape
    scale = 1.0 / count
    if depth % 8 or width % 128:
        pieces = [piece[:, :, start : start + depth] for piece in pieces]
        estimate = sectors_of(pieces, hosts, place, flip) * scale
        expected = jnp.maximum(estimate + measured[:, :, 1], 1.0)
        return spectrum_of(measured[:, :, 0] / expected * scale, owners, place, flip)

    def kernel(scalars, *refs):
        in_refs, measured_ref = refs[:owners], refs[owners]
        out_refs, held = refs[owners + 1 : 2 * owners + 1], refs[2 * owners + 1]

        def body(lanes):
            def emit(s, value):
                host, row = s // local, s % local
                expected = jnp.maximum(value * scale + measured_ref[host, 0, 1, row, :, lanes], 1.0)
                held[s] = measured_ref[host, 0, 0, row, :, lanes] / expected * scale

            gather_pieces(in_refs, held, scalars[1], lanes)
            synthesise(load_slots(held, count, scalars[0]), emit, 0, 1, count)
            spectrum = analyse(lambda s: held[s], 0, 1, count)
            store_slots(held, spectrum, scalars[0])
            scatter_pieces(out_refs, held, scalars[1], lanes)

        each_lane_tile(width, body)

    shape = (reals, parts, depth, width)
    specs = [piece_block(pieces[0].shape, start // 8)] * owners
    specs.append(pl.BlockSpec((hosts, 1, 2, local, 8, width), lambda c, t, _: (0, c, 0, 0, t, 0)))
    return tiles_call(
        kernel,
        [flip, place],
        (parts, depth // 8),
        [*pieces, measured],
        specs,
        [shape] * owners,
        [piece_block(shape)] * owners,
        count,
    )


def masked_block(system, pattern, which):
    _, _, _, height, width = system.shape
    rows, cols = pattern.shape[2:]
    tile_height, tile_width = height // rows, width // cols

    def kernel(which_ref, pattern_ref, in_ref, out_ref):
        for row in range(rows):
            for col in range(cols):
                at = (slice(row * tile_height, (row + 1) * tile_height),)
                at += (slice(col * tile_width, (col + 1) * tile_width),)
                value = pattern_ref[(which_ref[0] * rows + row) * cols + col].astype(jnp.float32)
                out_ref[(0,) + at] = in_ref[(0, 0, 0) + at] * value

    return pl.pallas_call(
        kernel,
        grid_spec=pltpu.PrefetchScalarGridSpec(
            num_scalar_prefetch=2,
            grid=(2,),
            in_specs=[pl.BlockSpec((1, 1, 1, height, width), lambda a, w, _: (0, w[0], a, 0, 0))],
            out_specs=pl.BlockSpec((1, height, width), lambda a, w, _: (a, 0, 0)),
        ),
        out_shape=jax.ShapeDtypeStruct((2, height, width), jnp.float32),
        cost_estimate=cost(2 * height * width, 16 * height * width),
        compiler_params=tile_params(1),
        name="masked",
    )(which.reshape(1), pattern.reshape(-1), system)


def split(value):
    high = value.astype(jnp.bfloat16)
    return high, (value - high.astype(jnp.float32)).astype(jnp.bfloat16)


def folded(first, second, weights):
    own, other, sign = weights[0], weights[1], weights[2]
    upper = own * first[0] + other * second[0]
    lower = other * first[0] + own * second[0]
    return upper, lower, sign * (first[1] - second[1])


def operator_of(first, second, weights, adjoint):
    height, inner = first.shape[1:]
    if height % 128 or inner % 128:
        upper, lower, cross = folded(first, second, weights)
        if adjoint:
            table = jnp.block([[upper, -cross], [cross, lower]])
        else:
            table = jnp.block([[upper.T, cross.T], [-cross.T, lower.T]])
        return split(table)
    shape = (2 * height, 2 * inner) if adjoint else (2 * inner, 2 * height)

    def kernel(weights_ref, first_ref, second_ref, high_ref, low_ref):
        def put(at, value):
            high_ref[at], low_ref[at] = split(value)

        index = pl.program_id(0)
        at = pl.ds(pl.multiple_of(index * 128, 128), 128)
        at2 = pl.ds(pl.multiple_of(index * 128 + height, 128), 128)
        upper, lower, cross = folded(first_ref, second_ref, weights_ref)
        one, two = slice(0, inner), slice(inner, 2 * inner)
        if adjoint:
            put((at, one), upper)
            put((at, two), -cross)
            put((at2, one), cross)
            put((at2, two), lower)
        else:
            cross = cross.T
            put((one, at), upper.T)
            put((one, at2), cross)
            put((two, at), -cross)
            put((two, at2), lower.T)

    return pl.pallas_call(
        kernel,
        grid_spec=pltpu.PrefetchScalarGridSpec(
            num_scalar_prefetch=1,
            grid=(height // 128,),
            in_specs=[pl.BlockSpec((2, 128, inner), lambda t, w: (0, t, 0))] * 2,
            out_specs=[pl.BlockSpec(shape, lambda t, w: (0, 0))] * 2,
        ),
        out_shape=[jax.ShapeDtypeStruct(shape, jnp.bfloat16)] * 2,
        compiler_params=tile_params(1),
        cost_estimate=cost(16 * height * inner, 32 * height * inner),
        name="operator",
    )(weights, first, second)


def apply_operators(operators, pieces):
    reals, parts, depth, width = pieces[0].shape
    slots, count = reals // 2, len(pieces)
    result = operators[0][0].shape[1] // 2
    if depth % 8 or width % 128 or result % 256:
        outs = []
        for piece in pieces:
            out = []
            for slot, (high, low) in enumerate(operators):
                table = high.astype(jnp.float32) + low.astype(jnp.float32)
                rows = jnp.concatenate([piece[2 * slot], piece[2 * slot + 1]], axis=-1)
                rows = jnp.einsum("cpi,ij->cpj", rows, table, precision=precise)
                out += [rows[..., :result], rows[..., result:]]
            outs.append(jnp.stack(out))
        return outs

    panel, per_part, rows = 256, result // 256, parts * depth
    group = max(1, min(count, 256 // rows))

    def kernel(*refs):
        terms, refs = refs[: 2 * slots], refs[2 * slots :]
        in_refs, out_refs, lhs_high, lhs_low = refs[:count], refs[count : 2 * count], *refs[2 * count :]

        @pl.when(pl.program_id(0) == 0)
        def _():
            for j in range(count):
                at = slice(j * rows, (j + 1) * rows)
                for slot in range(slots):
                    for part in range(2):
                        lanes = slice(part * width, (part + 1) * width)
                        high, low = split(in_refs[j][2 * slot + part].reshape(rows, width))
                        lhs_high[slot, at, lanes] = high
                        lhs_low[slot, at, lanes] = low

        dot = functools.partial(jnp.dot, preferred_element_type=jnp.float32)
        for first in range(0, count, group):
            last = min(first + group, count)
            at = slice(first * rows, last * rows)
            for slot in range(slots):
                high, low = terms[2 * slot][...], terms[2 * slot + 1][...]
                total = dot(lhs_high[slot, at, :], low) + dot(lhs_low[slot, at, :], high)
                total = total + dot(lhs_high[slot, at, :], high)
                for j in range(first, last):
                    value = total[(j - first) * rows : (j - first + 1) * rows]
                    out_refs[j][slot, 0] = value.reshape(parts, depth, panel)

    shape = (slots, 2, parts, depth, result)
    out_block = pl.BlockSpec(
        (slots, 1, parts, depth, panel), lambda t: (0, t // per_part, 0, 0, t % per_part)
    )
    outs = pl.pallas_call(
        kernel,
        grid=(2 * per_part,),
        in_specs=[pl.BlockSpec((2 * width, panel), lambda t: (0, t))] * (2 * slots)
        + [pl.BlockSpec(pieces[0].shape, lambda t: (0, 0, 0, 0))] * count,
        out_specs=[out_block] * count,
        out_shape=[jax.ShapeDtypeStruct(shape, jnp.float32)] * count,
        scratch_shapes=[pltpu.VMEM((slots, count * rows, 2 * width), jnp.bfloat16)] * 2,
        compiler_params=tile_params(1),
        cost_estimate=cost(24 * slots * count * rows * width * result, 3 * 2**23),
    )(*[term for pair in operators for term in pair], *pieces)
    return [out.reshape(reals, parts, depth, result) for out in outs]


def upper_side(side, sides):
    return 2 * side >= sides


def routes(count, hosts, sides):
    local, slots, half = count // hosts, count // 2 // hosts, count // 2
    within = hosts // sides
    rounds = []
    for slot in range(slots):
        for turn in range(2):
            sent, direct, inside = [None] * (hosts * sides), [], []
            for g in range(sides):
                for i in range(hosts):
                    r = slots * i + slot
                    near, far = r, (count - r if r else half)
                    upper = upper_side(g, sides)
                    if upper:
                        near, far = half + r, (half - r) % half
                    is_far = (i + turn + g + upper) % 2
                    k = far if is_far else near
                    host = k // local
                    source, origin, place = host * sides + g, host // within, i
                    if is_far:
                        place = (i + hosts // 2) % hosts
                    assert sent[source] is None
                    sent[source] = k % local
                    direct.append((source, g * hosts + i))
                    inside.append((source, origin * hosts + place))
            rounds.append((sent, direct, inside))
    return rounds


def on_device(hosts, sides, activity, system, pattern, counts, background, sensitivity):
    local, frames, planes, image = activity.shape
    sino = system.shape[3]
    count = local * hosts
    slots = count // 2 // hosts
    share = planes // sides
    depth = frames * share // hosts
    device = lax.axis_index(BOTH)
    seg = lax.axis_index("seg")
    side, place = device // hosts, device % hosts
    flip = upper_side(side, sides).astype(jnp.int32)
    chunks = 2 if depth % 16 == 0 else 1
    rows = depth // chunks

    def permute(array, pairs):
        return lax.ppermute(array, BOTH, pairs)

    def exchange_all(array):
        return lax.all_to_all(array, BOTH, split_axis=0, concat_axis=0, tiled=True)

    def shifted(pieces, sign):
        moved = list(pieces[:1])
        for j, piece in enumerate(pieces[1:], 1):
            pairs = [
                (a, a // hosts * hosts + (a + sign * j) % hosts) for a in range(sides * hosts)
            ]
            moved.append(permute(piece, pairs))
        return moved

    current = lax.dynamic_slice_in_dim(activity, seg * share, share, 2)
    columns = current.reshape(local, hosts, depth, image).transpose(1, 0, 2, 3)
    columns = jnp.broadcast_to(columns[None], (sides,) + columns.shape)
    columns = exchange_all(columns.reshape(sides * hosts, local, depth, image))
    columns = columns.reshape(hosts, sides, local, depth, image)

    measured = jnp.stack([counts[0].astype(jnp.float32), background[0]])
    measured = measured.reshape(2, local, frames, sides, share, sino).transpose(3, 0, 1, 2, 4, 5)
    measured = measured.reshape(sides, 2, local, hosts, depth, sino).transpose(0, 3, 1, 2, 4, 5)
    if sides == 2:
        kept = lax.dynamic_index_in_dim(measured, seg, keepdims=False)
        given = lax.dynamic_index_in_dim(measured, 1 - seg, keepdims=False)
        given = lax.ppermute(given, "seg", [(0, 1), (1, 0)])
        first = seg == 0
        measured = jnp.stack([jnp.where(first, kept, given), jnp.where(first, given, kept)])
    else:
        measured = lax.all_to_all(measured, "seg", split_axis=0, concat_axis=0, tiled=True)
    measured = measured.reshape(sides * hosts, 2, local, depth, sino)
    measured = [measured[:, :, :, m * rows : (m + 1) * rows] for m in range(chunks)]

    tables = routes(count, hosts, sides)
    masked = [
        masked_block(system, pattern, jnp.asarray(sent, jnp.int32)[device])
        for sent, _, _ in tables
    ]
    zero = slots * place + jnp.arange(slots) == 0
    if sides == 2:
        moved = []
        for turn, (_, _, inside) in enumerate(tables):
            pairs = [pair for pair in inside if pair[0] != pair[1]]
            stays = [0] * (hosts * sides)
            for source, target in inside:
                stays[target] = int(source == target)
            got = permute(masked[turn], pairs)
            moved.append(jnp.where(jnp.asarray(stays)[device] == 1, masked[turn], got))
        near, far = [], []
        for slot in range(slots):
            got = moved[2 * slot : 2 * slot + 2]
            near.append(jnp.where(seg == 0, got[0], got[1]))
            far.append(jnp.where(seg == 0, got[1], got[0]))
        across = []
        for i in range(hosts):
            other = (i + hosts // 2) % hosts
            across += [(other, hosts + i), (hosts + other, i)]
        far = [permute(block, across) for block in far]
        far, measured = lax.optimization_barrier((far, measured))
        blocks = list(zip(near, far))
        odd = flip
    else:
        moved = [lax.ppermute(block, BOTH, table[1]) for block, table in zip(masked, tables)]
        blocks = [moved[2 * slot : 2 * slot + 2] for slot in range(slots)]
        odd = (place + side) % 2
    measured = [
        exchange_all(array).reshape(hosts, sides, 2, local, rows, sino)
        for array in measured
    ]
    own = jnp.where(zero & (odd == 1), 0.0, 1.0)
    other = jnp.where(zero & (odd == 0), 0.0, 1.0)
    sign = jnp.where(zero, 0.0, 1.0 - 2.0 * odd)
    weights = jnp.stack([own, other, sign], axis=1)
    blocks = [(*pair, weights[slot]) for slot, pair in enumerate(blocks)]

    spectra = spectrum_of(columns, hosts, place, flip)
    spectra = shifted(spectra, 1)
    project = [operator_of(*block, False) for block in blocks]
    forward = apply_operators(project, spectra)
    forward = shifted(forward, -1)
    adjoint = [operator_of(*block, True) for block in blocks]
    totals = []
    for m, array in enumerate(measured):
        ratio = ratio_of(forward, array, m * rows, place, flip)
        ratio = shifted(ratio, 1)
        backward = apply_operators(adjoint, ratio)
        backward = shifted(backward, -1)
        back = sectors_of(backward, hosts, place, flip)
        back = exchange_all(back.reshape(hosts * sides, local, rows, image))
        totals.append(back.reshape(sides, hosts, local, rows, image).sum(0).transpose(1, 0, 2, 3))
    total = jnp.stack(totals, axis=2).reshape(local, frames, share, image)
    return current * total / sensitivity[:, None]


def solution(mesh):
    in_specs = (
        P("freq", None, None, None),
        P("seg", "freq", None, None, None),
        P("seg", "freq", None, None),
        P("seg", "freq", None, None, None),
        P("seg", "freq", None, None, None),
        P("freq", "seg", None),
    )
    hosts, sides = mesh.shape["freq"], mesh.shape["seg"]

    def body(activity, *rest):
        return on_device(hosts, sides, activity, *rest)

    return jax.shard_map(
        body, mesh=mesh, in_specs=in_specs, out_specs=P("freq", None, "seg", None), check_vma=False
    )
```
